256 devices in a mesh: shot: 16 (over z, core), pen: 16 (over y, x).
Axes of the slice: x: 4, y: 4, z: 8, core: 2. Of those that a mesh axis runs over, the one named last changes fastest.
Arguments:
- courant: float32 [16, 1024, 128], P('pen'), may hold values from 0.08 to 0.3
- source_states: float32 [16, 2, 16, 1024, 128], P('shot', None, 'pen'), may hold values from -6 to 6
- adjoint_states: float32 [16, 2, 16, 1024, 128], P('shot', None, 'pen'), may hold values from -6 to 6
- strips: float32 [16, 3, 2, 16, 2, 128], P('shot', None, None, 'pen'), may hold values from -6 to 6
- aperture: int32 [16, 2], P('shot'), may hold values from 0 to 7, as said below
- source_cell: int32 [16, 3], P('shot'), may hold values from 0 to 1023, as said below
- wavelet: float32 [16, 3], P('shot'), may hold values from -12 to 12
- receiver_cells: int32 [16, 512, 2], P('shot'), may hold values from 0 to 1023, as said below
- residuals: float32 [16, 3, 512], P('shot'), may hold values from -12 to 12
Outputs:
- precond: float32 [16, 1024, 128], P('pen', 'shot')
- smooth: float32 [16, 1024, 128], P('pen', 'shot')
The draws below stay inside these ranges and needn't reach their ends.
Inputs may be any that keep to these rules, and one draw needn't show every extreme that they name: `aperture`: row s is [first tile, number of tiles] of shot s along the second dimension in tiles of 128 cells; first tile + number of tiles <= 8, the number of tiles is 1 to 6, and some shot has exactly 6 tiles. `source_cell`: row s is [first, second, third] index of shot s's source within the grid; its second index lies inside the shot's aperture. `receiver_cells`: [first, second] index of each receiver within the grid, at depth index 2; the second index lies inside the shot's aperture.
All inputs are finite; a program needn't handle non-finite values.
Results may differ from the reference program's by a relative error of at most 0.0003.
Values sent between devices are 32-bit elements; how exact they have to be, the bound alone decides.
A program may use at most 64 MiB of HBM per device.

```python
import math
import jax
import jax.numpy as jnp
from jax import lax

TILE = 128
NTILES = 8
NZ = 128
AMAX = 6
STEPS = 3
SW = 2
NREC = 512
NY = 1024
NX = 16
SHOTS = 16
N_SHOT = 16


def aperture_layout(key):
    base_key = jax.random.fold_in(key, 11)
    key_list = jax.random.split(base_key, 3)
    shot_order = jnp.arange(SHOTS, dtype=jnp.int32)
    widest = jax.random.randint(key_list[0], (), 0, SHOTS)
    corner = (widest + 1) % SHOTS
    tile_counts = jax.random.randint(key_list[1], (SHOTS,), 1, 3)
    tile_counts = jnp.where(shot_order == widest, AMAX, jnp.where(shot_order == corner, 1, tile_counts))
    offsets = jax.random.randint(key_list[2], (SHOTS,), 0, NTILES - tile_counts + 1)
    offsets = jnp.where(shot_order == widest, 0, jnp.where(shot_order == corner, NTILES - 1, offsets))
    return (offsets.astype(jnp.int32), tile_counts.astype(jnp.int32), widest, corner)


def draw_aperture(key, part):
    offsets, tile_counts, widest, corner = aperture_layout(key)
    return jnp.stack([offsets, tile_counts], 1)


def draw_source_cell(key, part):
    offsets, tile_counts, widest, corner = aperture_layout(key)
    shot_order = jnp.arange(SHOTS, dtype=jnp.int32)
    key_list = jax.random.split(jax.random.fold_in(key, 23), 3)
    along_x = jax.random.randint(key_list[0], (SHOTS,), 0, NX)
    along_x = jnp.where(shot_order == widest, 0, along_x)
    along_y = offsets * TILE + jax.random.randint(key_list[1], (SHOTS,), 0, tile_counts * TILE)
    along_y = jnp.where(shot_order == corner, NY - 1, along_y)
    along_z = jax.random.randint(key_list[2], (SHOTS,), 0, NZ)
    return jnp.stack([along_x, along_y, along_z], 1).astype(jnp.int32)


def draw_receiver_cells(key, part):
    offsets, tile_counts, widest, corner = aperture_layout(key)
    shot_order = jnp.arange(SHOTS, dtype=jnp.int32)
    first_slot = (jnp.arange(NREC, dtype=jnp.int32) == 0)[None, :]
    key_list = jax.random.split(jax.random.fold_in(key, 37), 2)
    along_x = jax.random.randint(key_list[0], (SHOTS, NREC), 0, NX)
    along_x = jnp.where((shot_order == widest)[:, None] & first_slot, 0, along_x)
    along_y = offsets[:, None] * TILE + jax.random.randint(key_list[1], (SHOTS, NREC), 0, (tile_counts * TILE)[:, None])
    along_y = jnp.where((shot_order == widest)[:, None] & first_slot, 0, along_y)
    along_y = jnp.where((shot_order == corner)[:, None] & first_slot, NY - 1, along_y)
    return jnp.stack([along_x, along_y], 2).astype(jnp.int32)


def block_levels(own_key, dims, shards, low, high):
    def one(dim, parts):
        heights = jax.random.uniform(jax.random.fold_in(jax.random.fold_in(own_key, 6), dim), (parts,), jnp.float32, low / len(shards), high / len(shards))
        return jnp.repeat(jnp.exp(heights), dims[dim] // parts).reshape((-1,) + (1,) * (len(dims) - dim - 1))

    gain = one(*shards[0])
    for cut in shards[1:]:
        gain = gain * one(*cut)
    return gain


def noise(own_key, dims, scale, reach, shards=(), kind=jnp.bfloat16):
    result = scale * jax.random.normal(own_key, dims, jnp.float32)
    if shards:
        result = result * block_levels(own_key, dims, shards, -0.22, 0.18)
    return jnp.clip(result, -reach, reach).astype(kind)


def setup_inputs(seed: int = 0) -> dict:
    seeds = jax.random.split(jax.random.key(seed), 10)
    courant = jnp.clip(jnp.exp(math.log(0.3) - 1.3217559 * jax.random.uniform(seeds[0], (NX, NY, NZ), jnp.float32) ** block_levels(seeds[0], (NX, NY, NZ), ((0, 16),), -0.2, 0.2)), 0.08, 0.3)
    source_states = noise(seeds[1], (SHOTS, 2, NX, NY, NZ), 1.0, 6.0, ((0, 16), (2, 16)), jnp.float32)
    adjoint_states = noise(seeds[2], (SHOTS, 2, NX, NY, NZ), 1.0, 6.0, ((0, 16), (2, 16)), jnp.float32)
    strips = noise(seeds[3], (SHOTS, STEPS, 2, NX, SW, NZ), 1.0, 6.0, ((0, 16), (3, 16)), jnp.float32)
    aperture = draw_aperture(jax.random.fold_in(seeds[9], 71), 0)
    source_cell = draw_source_cell(jax.random.fold_in(seeds[9], 71), 0)
    wavelet = noise(seeds[6], (SHOTS, STEPS), 4.0, 12.0, ((0, 16),), jnp.float32)
    receiver_cells = draw_receiver_cells(jax.random.fold_in(seeds[9], 71), 0)
    residuals = noise(seeds[8], (SHOTS, STEPS, NREC), 2.0, 12.0, ((0, 16),), jnp.float32)
    return dict(courant=courant, source_states=source_states, adjoint_states=adjoint_states, strips=strips, aperture=aperture, source_cell=source_cell, wavelet=wavelet, receiver_cells=receiver_cells, residuals=residuals)


receiver_depth = 2
damping = 1.0
sigma_z = 4.0

def laplace(wavefield):
    padded = jnp.pad(wavefield, 1)
    beside = padded[2:, 1:-1, 1:-1] + padded[:-2, 1:-1, 1:-1]
    beside = beside + padded[1:-1, 2:, 1:-1] + padded[1:-1, :-2, 1:-1]
    beside = beside + padded[1:-1, 1:-1, 2:] + padded[1:-1, 1:-1, :-2]
    return beside - 6.0 * wavefield

def response(length, spread):
    frequency = jnp.fft.fftfreq(length)
    return jnp.exp(-0.5 * (spread * 2.0 * math.pi * frequency) ** 2)

def gauss_block(total, spread):
    position = jnp.arange(total, dtype=jnp.int32)
    distance = (position[:, None] - position[None, :]).astype(jnp.float32)
    return jnp.exp(-0.5 * (distance / spread) ** 2) / (spread * math.sqrt(2.0 * math.pi))

def reference(courant, source_states, adjoint_states, strips, aperture, source_cell, wavelet, receiver_cells, residuals):
    row_index = jnp.arange(NY, dtype=jnp.int32)
    anchor = jnp.zeros((), jnp.int32)

    def one_shot(totals, shot_item):
        gradient_sum, lighting_sum = totals
        source_pair, adjoint_pair, strip_set, aperture_row, source_row, amplitude, receivers, traces = shot_item
        box_low = aperture_row[0] * TILE
        box_high = (aperture_row[0] + aperture_row[1]) * TILE
        inside_box = ((row_index >= box_low) & (row_index < box_high)).astype(jnp.float32)[None, :, None]
        source_now = source_pair[0] * inside_box
        source_next = source_pair[1] * inside_box
        adjoint_now = adjoint_pair[0] * inside_box
        adjoint_next = adjoint_pair[1] * inside_box
        source_gain = courant[source_row[0], source_row[1], source_row[2]]
        receiver_gain = courant[receivers[:, 0], receivers[:, 1], receiver_depth]
        gradient = jnp.zeros(courant.shape, jnp.float32)
        lighting = jnp.zeros(courant.shape, jnp.float32)
        for moment in range(STEPS):
            source_prev = 2.0 * source_now - source_next + courant * laplace(source_now)
            source_prev = source_prev.at[source_row[0], source_row[1], source_row[2]].add(source_gain * amplitude[moment])
            source_prev = source_prev * inside_box
            source_prev = lax.dynamic_update_slice(source_prev, strip_set[moment, 0], (anchor, box_low, anchor))
            source_prev = lax.dynamic_update_slice(source_prev, strip_set[moment, 1], (anchor, box_high - SW, anchor))
            adjoint_prev = 2.0 * adjoint_now - adjoint_next + courant * laplace(adjoint_now)
            adjoint_prev = adjoint_prev.at[receivers[:, 0], receivers[:, 1], receiver_depth].add(receiver_gain * traces[moment])
            adjoint_prev = adjoint_prev * inside_box
            gradient = gradient + (source_next - 2.0 * source_now + source_prev) * adjoint_now
            lighting = lighting + source_now * source_now
            source_next, source_now = (source_now, source_prev)
            adjoint_next, adjoint_now = (adjoint_now, adjoint_prev)
        return ((gradient_sum + gradient, lighting_sum + lighting), None)
    empty_grid = jnp.zeros(courant.shape, jnp.float32)
    sums, unused = lax.scan(one_shot, (empty_grid, empty_grid), (source_states, adjoint_states, strips, aperture, source_cell, wavelet, receiver_cells, residuals))
    precond = sums[0] / (sums[1] + damping)
    sigma_y = float(NY) / float(N_SHOT)
    spectrum = response(NY, sigma_y)[None, :, None] * response(NZ, sigma_z)[None, None, :]
    filtered = jnp.real(jnp.fft.ifftn(jnp.fft.fftn(precond, axes=(1, 2)) * spectrum, axes=(1, 2))).astype(jnp.float32)
    x_matrix = gauss_block(NX, float(NX) / 4.0)
    smooth = jnp.einsum('ab,byz->ayz', x_matrix, filtered, precision=lax.Precision.HIGHEST)
    return (precond, smooth)
```

```python
import math

import jax
import jax.numpy as jnp
import numpy as np
from jax import lax
from jax.sharding import PartitionSpec as P

TILE = 128
SW = 2
NY = 1024


receiver_depth = 2
damping = 1.0
sigma_z = 4.0
highest = lax.Precision.HIGHEST


def padded_2(block, sides, width):
    for axis, dim in sides:
        count = lax.axis_size(axis)
        forward = [(i, i + 1) for i in range(count - 1)]
        backward = [(target, source) for source, target in forward]
        low = lax.ppermute(
            lax.slice_in_dim(block, block.shape[dim] - width, None, axis=dim), axis, forward
        )
        high = lax.ppermute(lax.slice_in_dim(block, 0, width, axis=dim), axis, backward)
        block = jnp.concatenate([low, block, high], axis=dim)
    return block


def circulant_table(length, spread):
    frequency = np.fft.fftfreq(length)
    weights = np.exp(-0.5 * (spread * 2.0 * np.pi * frequency) ** 2)
    vector = np.real(np.fft.ifft(weights))
    position = np.arange(length)
    return vector[(position[:, None] - position[None, :]) % length].astype(np.float32)


def wave_table(length, spread):
    half = 64
    order = np.concatenate([np.arange(half), np.arange(1, half + 1)])
    angle = 2.0 * np.pi * ((order[:, None] * np.arange(length)[None, :]) % length) / length
    waves = np.where(np.arange(2 * half)[:, None] < half, np.cos(angle), np.sin(angle))
    weights = np.exp(-0.5 * (spread * 2.0 * np.pi * order / length) ** 2) / length
    weights = np.where(order == 0, weights, 2.0 * weights)
    return waves.astype(np.float32), weights.astype(np.float32)


def gauss_table(total, spread):
    position = np.arange(total)
    distance = (position[:, None] - position[None, :]).astype(np.float64)
    table = np.exp(-0.5 * (distance / spread) ** 2) / (spread * math.sqrt(2.0 * math.pi))
    return table.astype(np.float32)


def laplace(state):
    padded = padded_2(state, (("pen", 1),), 1)
    beside = padded[:, 2:] + padded[:, :-2]
    side_y = jnp.pad(state, ((0, 0), (0, 0), (1, 1), (0, 0)))
    beside = beside + side_y[:, :, 2:] + side_y[:, :, :-2]
    side_z = jnp.pad(state, ((0, 0), (0, 0), (0, 0), (1, 1)))
    beside = beside + side_z[:, :, :, 2:] + side_z[:, :, :, :-2]
    return beside - 6.0 * state


def on_device(
    courant,
    source_states,
    adjoint_states,
    strips,
    aperture,
    source_cell,
    wavelet,
    receiver_cells,
    residuals,
):
    planes = courant.shape[0]
    z_cells = courant.shape[2]
    first_x = lax.axis_index("pen") * planes
    anchor = jnp.zeros((), jnp.int32)
    offsets = aperture[0, 0]
    box_tiles = aperture[0, 1]
    box_low = offsets * TILE
    box_high = (offsets + box_tiles) * TILE
    window_width = NY
    current = jnp.stack([source_states[0, 0], adjoint_states[0, 0]])
    following = jnp.stack([source_states[0, 1], adjoint_states[0, 1]])
    row_index = jnp.arange(window_width, dtype=jnp.int32)
    inside_box = ((row_index >= box_low) & (row_index < box_high)).astype(jnp.float32)[
        None, :, None
    ]
    current = current * inside_box[None]
    following = following * inside_box[None]
    plane_index = first_x + jnp.arange(planes, dtype=jnp.int32)
    depth_index = jnp.arange(z_cells, dtype=jnp.int32)
    source_hit = (
        (plane_index[:, None, None] == source_cell[0, 0])
        & (row_index[None, :, None] == source_cell[0, 1])
        & (depth_index[None, None, :] == source_cell[0, 2])
    )
    source_term = jnp.where(source_hit, courant, 0.0)
    receiver_x = receiver_cells[0, :, 0] - first_x
    receiver_y = receiver_cells[0, :, 1]
    usable = (
        (receiver_x >= 0) & (receiver_x < planes) & (receiver_y >= 0) & (receiver_y < window_width)
    )
    flat_cell = jnp.where(usable, receiver_x * window_width + receiver_y, -1)
    selector = (
        flat_cell[:, None] == jnp.arange(planes * window_width, dtype=jnp.int32)[None, :]
    ).astype(jnp.float32)
    step_count = residuals.shape[1]
    injected = jnp.dot(residuals[0], selector, precision=highest).reshape(
        step_count, planes, window_width
    )
    receiver_gain = courant[:, :, receiver_depth]
    gradient = jnp.zeros((planes, window_width, z_cells), jnp.float32)
    lighting = jnp.zeros((planes, window_width, z_cells), jnp.float32)
    for moment in range(step_count):
        last = moment == step_count - 1
        if last:
            previous = 2.0 * current[:1] - following[:1] + courant[None] * laplace(current[:1])
        else:
            previous = 2.0 * current - following + courant[None] * laplace(current)
        source_prev = previous[0] + wavelet[0, moment] * source_term
        source_prev = source_prev * inside_box
        source_prev = lax.dynamic_update_slice(
            source_prev, strips[0, moment, 0], (anchor, box_low, anchor)
        )
        source_prev = lax.dynamic_update_slice(
            source_prev, strips[0, moment, 1], (anchor, box_high - SW, anchor)
        )
        gradient = gradient + (following[0] - 2.0 * current[0] + source_prev) * current[1]
        lighting = lighting + current[0] * current[0]
        if last:
            break
        adjoint_prev = previous[1].at[:, :, receiver_depth].add(injected[moment] * receiver_gain)
        adjoint_prev = adjoint_prev * inside_box
        following = current
        current = jnp.stack([source_prev, adjoint_prev])
    groups = lax.axis_size("shot")
    share_rows = NY // groups
    shot_here = lax.axis_index("shot")
    both = jnp.stack([gradient[0], lighting[0]])
    both = lax.psum_scatter(both, "shot", scatter_dimension=1, tiled=True)
    precond = both[0] / (both[1] + damping)
    z_matrix = circulant_table(z_cells, sigma_z)
    smooth_z = jnp.dot(precond, z_matrix, precision=highest)
    column = lax.all_gather(smooth_z, "shot", axis=0, tiled=True)
    waves, weights = wave_table(NY, float(NY) / float(groups))
    waves_here = lax.dynamic_slice_in_dim(jnp.asarray(waves), shot_here * share_rows, share_rows, 1)
    amount = jnp.dot(waves, column, precision=highest) * weights[:, None]
    smooth_y = jnp.dot(waves_here.T, amount, precision=highest)
    pen_count = lax.axis_size("pen")
    total_x = planes * pen_count
    x_table = gauss_table(total_x, float(total_x) / 4.0)
    x_row = lax.dynamic_index_in_dim(jnp.asarray(x_table), lax.axis_index("pen"), 0, keepdims=False)
    all_planes = lax.all_gather(smooth_y, "pen", axis=0, tiled=False)
    smooth = jnp.sum(all_planes * x_row[:, None, None], axis=0)
    return (precond[None], smooth[None])


def solution(mesh):
    placed = (
        P("pen", None, None),
        P("shot", None, "pen", None, None),
        P("shot", None, "pen", None, None),
        P("shot", None, None, "pen", None, None),
        P("shot", None),
        P("shot", None),
        P("shot", None),
        P("shot", None, None),
        P("shot", None, None),
    )
    return jax.shard_map(
        on_device,
        mesh=mesh,
        in_specs=placed,
        out_specs=(P("pen", "shot", None), P("pen", "shot", None)),
        check_vma=False,
    )
```

```python
import math

import jax
import jax.numpy as jnp
import numpy as np
from jax import lax
from jax.experimental import pallas as pl
from jax.experimental.pallas import tpu as pltpu
from jax.sharding import PartitionSpec as P

TILE = 128
NY = 1024
NZ = 128
AMAX = 6
STEPS = 3
NREC = 512
SHOTS = 16
PLANES = 16
ROWS = AMAX * TILE
CHUNK = NY // SHOTS
MODES = 128
DEPTH = 2
SHIFTS = NY // TILE - AMAX + 1
DAMPING = 1.0
SIGMA_Z = 4.0
MESH = pl.DeviceIdType.MESH
HIGHEST = lax.Precision.HIGHEST
LAYERS = 8
SIDE = 4
PEN_REL = [(dy, dx) for dy in range(SIDE) for dx in range(SIDE) if (dy, dx) != (0, 0)]
SHOT_REL = [(dz, dc) for dz in range(LAYERS) for dc in range(2) if (dz, dc) != (0, 0)]


def wave_table(length, spread):
    half = MODES // 2
    order = np.concatenate([np.arange(half), np.arange(1, half + 1)])
    angle = 2.0 * np.pi * ((order[:, None] * np.arange(length)[None, :]) % length) / length
    waves = np.where(np.arange(2 * half)[:, None] < half, np.cos(angle), np.sin(angle))
    weights = np.exp(-0.5 * (spread * 2.0 * np.pi * order / length) ** 2) / length
    weights = np.where(order == 0, weights, 2.0 * weights)
    plain = waves.T.reshape(SHOTS, CHUNK, MODES)
    scaled = (waves * weights[:, None]).T.reshape(SHOTS, CHUNK, MODES)
    return plain.astype(np.float32), scaled.astype(np.float32)


def circulant_table(length, spread):
    frequency = np.fft.fftfreq(length)
    weights = np.exp(-0.5 * (spread * 2.0 * np.pi * frequency) ** 2)
    vector = np.real(np.fft.ifft(weights))
    position = np.arange(length)
    return vector[(position[:, None] - position[None, :]) % length].astype(np.float32)


def gauss_table(total, spread):
    position = np.arange(total)
    distance = (position[:, None] - position[None, :]).astype(np.float64)
    table = np.exp(-0.5 * (distance / spread) ** 2) / (spread * math.sqrt(2.0 * math.pi))
    return table.astype(np.float32)


def block_rows(b, pad=0):
    return pl.ds(pl.multiple_of(b * TILE + pad, 8), TILE)


def kernel(
    aperture,
    source_cell,
    wavelet,
    gauss,
    courant,
    source,
    adjoint,
    strips,
    cells,
    residuals,
    z_table,
    plain,
    scaled,
    precond_out,
    smooth_out,
    ua,
    ub,
    ra,
    rb,
    cw,
    hit,
    inj,
    from_low,
    from_high,
    grad,
    light,
    split_g,
    split_l,
    pair_g,
    pair_l,
    mine_g,
    mine_l,
    ring_g,
    ring_l,
    part,
    part_in,
    coef,
    coef_in,
    total,
    halo_send,
    halo_recv,
    pair_send,
    pair_recv,
    ring_send,
    ring_recv,
    part_send,
    part_recv,
    coef_send,
    coef_recv,
    total_send,
    total_recv,
):
    shot = lax.axis_index("shot")
    pen = lax.axis_index("pen")
    z, core = shot // 2, lax.rem(shot, 2)
    py, px = pen // SIDE, lax.rem(pen, SIDE)

    def pen_peer(rel):
        dy, dx = rel
        return (shot, lax.rem(py + dy, SIDE) * SIDE + lax.rem(px + dx, SIDE))

    def shot_peer(rel):
        dz, dc = rel
        return lax.rem(z + dz, LAYERS) * 2 + lax.rem(core + dc, 2)

    barrier = pltpu.get_barrier_semaphore()
    for rel in PEN_REL:
        pl.semaphore_signal(barrier, inc=1, device_id=pen_peer(rel), device_id_type=MESH)
    for rel in SHOT_REL:
        pl.semaphore_signal(
            barrier, inc=1, device_id=(shot_peer(rel), pen), device_id_type=MESH
        )

    first = aperture[0, 0]
    count = aperture[0, 1]
    window = jnp.minimum(first, NY // TILE - AMAX)
    low = first - window
    high = low + count
    start = window * TILE

    edge = jnp.zeros((8, NZ), jnp.float32)
    for ref in (ua, ub, ra, rb):
        ref[pl.ds(0, 8), :] = edge
        ref[pl.ds(ROWS + 8, 8), :] = edge

    lane = lax.broadcasted_iota(jnp.int32, (TILE, NZ), 1)
    row = lax.broadcasted_iota(jnp.int32, (TILE, NZ), 0)

    def pick(options, like):
        where_from = like * 0 + window
        out = options[SHIFTS - 1]
        for i in range(SHIFTS - 2, -1, -1):
            out = jnp.where(where_from == i, options[i], out)
        return out

    def load_block(b, carry):
        row_here = row + b * TILE
        inside = (row_here >= low * TILE) & (row_here < high * TILE)
        here = block_rows(b, 8)

        def take(ref, *lead):
            options = [ref[(*lead, block_rows(b, i * TILE))] for i in range(SHIFTS)]
            return jnp.where(inside, pick(options, row), 0.0)

        ua[here, :] = take(source, 0)
        ub[here, :] = take(source, 1)
        ra[here, :] = take(adjoint, 0)
        rb[here, :] = take(adjoint, 1)
        cw[block_rows(b), :] = take(courant)
        return carry

    lax.fori_loop(0, AMAX, load_block, 0)

    @pl.when(pen == 0)
    def _():
        from_low[...] = jnp.zeros_like(from_low)

    @pl.when(pen == PLANES - 1)
    def _():
        from_high[...] = jnp.zeros_like(from_high)

    pl.semaphore_wait(barrier, len(PEN_REL) + len(SHOT_REL))

    up = (shot, lax.rem(pen + 1, PLANES))
    down = (shot, lax.rem(pen + PLANES - 1, PLANES))

    def halo(state, slot):
        body = state.at[pl.ds(8, ROWS), :]
        upward = pltpu.make_async_remote_copy(
            body, from_low.at[slot], halo_send.at[slot, 0], halo_recv.at[slot, 0],
            device_id=up, device_id_type=MESH,
        )
        downward = pltpu.make_async_remote_copy(
            body, from_high.at[slot], halo_send.at[slot, 1], halo_recv.at[slot, 1],
            device_id=down, device_id_type=MESH,
        )

        class Pair:
            def start(self):
                pl.when(pen < PLANES - 1)(upward.start)
                pl.when(pen > 0)(downward.start)

            def sent(self):
                pl.when(pen < PLANES - 1)(upward.wait_send)
                pl.when(pen > 0)(downward.wait_send)

            def arrived(self):
                pl.when(pen > 0)(upward.wait_recv)
                pl.when(pen < PLANES - 1)(downward.wait_recv)

        return Pair()

    not_first = lane > 0
    not_last = lane < NZ - 1

    def laplace(state, slot, b):
        wide = state[pl.ds(pl.multiple_of(b * TILE, TILE), TILE + 16), :]
        here = wide[8 : TILE + 8]
        at = block_rows(b)
        beside = from_low[slot, at, :] + from_high[slot, at, :]
        beside = beside + pltpu.roll(wide, 1, 0)[8 : TILE + 8]
        beside = beside + pltpu.roll(wide, TILE + 15, 0)[8 : TILE + 8]
        beside = beside + jnp.where(not_first, pltpu.roll(here, 1, 1), 0.0)
        beside = beside + jnp.where(not_last, pltpu.roll(here, NZ - 1, 1), 0.0)
        return here, beside - 6.0 * here

    def source_step(now, old, slot, moment, adjoint_now, last):
        amplitude = wavelet[0, moment]

        def body(b, carry):
            here, lap = laplace(now, slot, b)
            at = block_rows(b)
            at8 = block_rows(b, 8)
            before = old[at8, :]
            new = 2.0 * here - before + cw[at, :] * (lap + amplitude * hit[at, :])
            row_here = row + b * TILE
            for i in range(2):
                new = jnp.where(
                    row_here == low * TILE + i, strips[moment, 0, pl.ds(i, 1), :], new
                )
                new = jnp.where(
                    row_here == high * TILE - 2 + i, strips[moment, 1, pl.ds(i, 1), :], new
                )
            at256 = block_rows(b, 2 * TILE)
            step = (before - 2.0 * here + new) * adjoint_now[at8, :]
            if moment == 0:
                grad[at256, :] = step
                light[at256, :] = here * here
            else:
                grad[at256, :] = grad[at256, :] + step
            if not last:
                old[at8, :] = new
            if moment < STEPS - 1 and moment > 0:
                light[at256, :] = light[at256, :] + here * here + new * new
            return carry

        lax.fori_loop(0, AMAX, body, 0)

    def adjoint_step(now, old, slot, moment):
        def body(b, carry):
            here, lap = laplace(now, slot, b)
            at = block_rows(b)
            at8 = block_rows(b, 8)
            old[at8, :] = 2.0 * here - old[at8, :] + cw[at, :] * (lap + inj[moment, at, :])
            return carry

        lax.fori_loop(0, AMAX, body, 0)

    u0, r0, u1, r1, u2 = halo(ua, 0), halo(ra, 1), halo(ub, 2), halo(rb, 3), halo(ua, 4)
    u0.start()

    cell_row = jnp.where(cells[pl.ds(0, 1), :] == pen, cells[pl.ds(1, 1), :] - start, -1)
    slab = lax.broadcasted_iota(jnp.int32, (2 * NZ, NREC), 0)
    values = jnp.where(
        slab == DEPTH,
        residuals[pl.ds(0, 1), :],
        jnp.where(slab == NZ + DEPTH, residuals[pl.ds(1, 1), :], 0.0),
    )
    fine = []
    for _ in range(3):
        piece = values.astype(jnp.bfloat16)
        values = values - piece.astype(jnp.float32)
        fine.append(piece)
    rows_wide = lax.broadcasted_iota(jnp.int32, (TILE, NREC), 0)

    def inject_block(b, carry):
        chosen = jnp.where(rows_wide == cell_row - b * TILE, 1.0, 0.0).astype(jnp.bfloat16)
        out = jnp.zeros((TILE, 2 * NZ), jnp.float32)
        for piece in fine:
            out = out + lax.dot_general(
                chosen, piece, (((1,), (1,)), ((), ())), preferred_element_type=jnp.float32
            )
        at = block_rows(b)
        inj[0, at, :] = out[:, :NZ]
        inj[1, at, :] = out[:, NZ:]
        key = row + (b * TILE + pen * NY)
        cell = source_cell[0, 0] * NY + source_cell[0, 1] - start
        here = (key == cell) & (lane == source_cell[0, 2])
        hit[at, :] = jnp.where(here, 1.0, 0.0)
        return carry

    lax.fori_loop(0, AMAX, inject_block, 0)
    for ref in (grad, light):
        ref[pl.ds(0, 2 * TILE), :] = jnp.zeros((2 * TILE, NZ), jnp.float32)
        ref[pl.ds(ROWS + 2 * TILE, 2 * TILE), :] = jnp.zeros((2 * TILE, NZ), jnp.float32)

    def spread(full, split):
        def body(i, carry):
            options = []
            for shift in range(SHIFTS):
                at = pl.multiple_of((SHIFTS - 1 - shift) * TILE + i * CHUNK, CHUNK)
                options.append(full[pl.ds(at, CHUNK), :])
            split[lax.rem(i, 2), i // 2] = pick(options, row[:CHUNK])
            return carry

        lax.fori_loop(0, SHOTS, body, 0)

    def to_pair(split, pair, k):
        return pltpu.make_async_remote_copy(
            split.at[1 - core], pair, pair_send.at[k], pair_recv.at[k],
            device_id=(2 * z + 1 - core, pen), device_id_type=MESH,
        )

    def to_ring(split, pair, mine, ring, k):
        mine[...] = split[core] + pair[...]
        copies = []
        for d in range(1, LAYERS):
            target = lax.rem(z + d, LAYERS)
            copies.append(
                pltpu.make_async_remote_copy(
                    mine.at[target], ring.at[d - 1], ring_send.at[k, d - 1],
                    ring_recv.at[k, d - 1],
                    device_id=(2 * target + core, pen), device_id_type=MESH,
                )
            )
        return copies

    u0.sent()
    r0.start()
    u0.arrived()
    source_step(ua, ub, 0, 0, ra, False)
    r0.sent()
    u1.start()
    r0.arrived()
    adjoint_step(ra, rb, 1, 0)
    u1.sent()
    r1.start()
    u1.arrived()
    source_step(ub, ua, 2, 1, rb, False)
    spread(light, split_l)
    pair_light = to_pair(split_l, pair_l, 0)
    pair_light.start()
    r1.sent()
    u2.start()
    pair_light.wait()
    ring_light = to_ring(split_l, pair_l, mine_l, ring_l, 0)
    for copy in ring_light:
        copy.start()
    r1.arrived()
    adjoint_step(rb, ra, 3, 1)
    u2.arrived()
    source_step(ua, ub, 4, 2, ra, True)
    spread(grad, split_g)
    pair_grad = to_pair(split_g, pair_g, 1)
    pair_grad.start()
    for copy in ring_light:
        copy.wait()
    lighting = mine_l[z]
    for d in range(LAYERS - 1):
        lighting = lighting + ring_l[d]
    u2.sent()
    pair_grad.wait()
    ring_grad = to_ring(split_g, pair_g, mine_g, ring_g, 1)
    for copy in ring_grad:
        copy.start()
    for copy in ring_grad:
        copy.wait()
    gradient = mine_g[z]
    for d in range(LAYERS - 1):
        gradient = gradient + ring_g[d]
    precond = gradient / (lighting + DAMPING)
    precond_out[...] = precond

    smooth_z = jnp.dot(
        precond, z_table[...], precision=HIGHEST, preferred_element_type=jnp.float32
    )
    partial = lax.dot_general(
        plain[shot], smooth_z, (((0,), (0,)), ((), ())), precision=HIGHEST,
        preferred_element_type=jnp.float32,
    )
    for s in range(SHOTS):
        part[s] = partial[8 * s : 8 * s + 8]
    copies = []
    for i, rel in enumerate(SHOT_REL):
        peer = shot_peer(rel)
        copies.append(
            pltpu.make_async_remote_copy(
                part.at[peer], part_in.at[i], part_send.at[i], part_recv.at[i],
                device_id=(peer, pen), device_id_type=MESH,
            )
        )
    for copy in copies:
        copy.start()
    for copy in copies:
        copy.wait()
    tally = part[shot]
    for i in range(len(SHOT_REL)):
        tally = tally + part_in[i]
    coef[...] = tally
    copies = []
    for i, rel in enumerate(PEN_REL):
        copies.append(
            pltpu.make_async_remote_copy(
                coef, coef_in.at[i], coef_send.at[i], coef_recv.at[i],
                device_id=pen_peer(rel), device_id_type=MESH,
            )
        )
    for copy in copies:
        copy.start()
    mixed = tally * gauss[pen, pen]
    for copy in copies:
        copy.wait()
    for i, (dy, dx) in enumerate(PEN_REL):
        origin = lax.rem(py + SIDE - dy, SIDE) * SIDE + lax.rem(px + SIDE - dx, SIDE)
        mixed = mixed + coef_in[i] * gauss[pen, origin]
    total[shot] = mixed
    copies = []
    for i, rel in enumerate(SHOT_REL):
        copies.append(
            pltpu.make_async_remote_copy(
                total.at[shot], total.at[shot], total_send.at[i], total_recv.at[i],
                device_id=(shot_peer(rel), pen), device_id_type=MESH,
            )
        )
    for copy in copies:
        copy.start()
    for copy in copies:
        copy.wait()
    smooth_out[...] = jnp.dot(
        scaled[shot], total[...].reshape(MODES, NZ), precision=HIGHEST,
        preferred_element_type=jnp.float32,
    )


def on_device(
    courant,
    source_states,
    adjoint_states,
    strips,
    aperture,
    source_cell,
    wavelet,
    receiver_cells,
    residuals,
):
    plain, scaled = wave_table(NY, float(NY) / float(SHOTS))
    vmem = pl.BlockSpec(memory_space=pltpu.VMEM)
    smem = pl.BlockSpec(memory_space=pltpu.SMEM)
    f32 = jnp.float32
    dma = pltpu.SemaphoreType.DMA
    others = SHOTS - 1
    state = pltpu.VMEM((ROWS + 16, NZ), f32)
    field = pltpu.VMEM((ROWS, NZ), f32)
    precond, smooth = pl.pallas_call(
        kernel,
        out_shape=[jax.ShapeDtypeStruct((CHUNK, NZ), f32)] * 2,
        in_specs=[smem] * 4 + [vmem] * 9,
        out_specs=[vmem, vmem],
        scratch_shapes=[
            state,
            state,
            state,
            state,
            field,
            field,
            pltpu.VMEM((2, ROWS, NZ), f32),
            pltpu.VMEM((5, ROWS, NZ), f32),
            pltpu.VMEM((5, ROWS, NZ), f32),
            pltpu.VMEM((ROWS + 4 * TILE, NZ), f32),
            pltpu.VMEM((ROWS + 4 * TILE, NZ), f32),
            pltpu.VMEM((2, LAYERS, CHUNK, NZ), f32),
            pltpu.VMEM((2, LAYERS, CHUNK, NZ), f32),
            pltpu.VMEM((LAYERS, CHUNK, NZ), f32),
            pltpu.VMEM((LAYERS, CHUNK, NZ), f32),
            pltpu.VMEM((LAYERS, CHUNK, NZ), f32),
            pltpu.VMEM((LAYERS, CHUNK, NZ), f32),
            pltpu.VMEM((LAYERS - 1, CHUNK, NZ), f32),
            pltpu.VMEM((LAYERS - 1, CHUNK, NZ), f32),
            pltpu.VMEM((SHOTS, 8, NZ), f32),
            pltpu.VMEM((others, 8, NZ), f32),
            pltpu.VMEM((8, NZ), f32),
            pltpu.VMEM((others, 8, NZ), f32),
            pltpu.VMEM((SHOTS, 8, NZ), f32),
            dma((5, 2)),
            dma((5, 2)),
            dma((2,)),
            dma((2,)),
            dma((2, LAYERS - 1)),
            dma((2, LAYERS - 1)),
            dma((others,)),
            dma((others,)),
            dma((others,)),
            dma((others,)),
            dma((others,)),
            dma((others,)),
        ],
        compiler_params=pltpu.CompilerParams(
            collective_id=0, has_side_effects=True, vmem_limit_bytes=48 << 20
        ),
        name="inversion",
    )(
        aperture,
        source_cell,
        wavelet,
        jnp.asarray(gauss_table(PLANES, float(PLANES) / 4.0)),
        courant[0],
        source_states[0, :, 0],
        adjoint_states[0, :, 0],
        strips[0, :, :, 0],
        receiver_cells[0].T,
        residuals[0],
        jnp.asarray(circulant_table(NZ, SIGMA_Z)),
        jnp.asarray(plain),
        jnp.asarray(scaled),
    )
    return (precond[None], smooth[None])


def solution(mesh):
    placed = (
        P("pen", None, None),
        P("shot", None, "pen", None, None),
        P("shot", None, "pen", None, None),
        P("shot", None, None, "pen", None, None),
        P("shot", None),
        P("shot", None),
        P("shot", None),
        P("shot", None, None),
        P("shot", None, None),
    )
    return jax.shard_map(
        on_device,
        mesh=mesh,
        in_specs=placed,
        out_specs=(P("pen", "shot", None), P("pen", "shot", None)),
        check_vma=False,
    )
```

```python
import math

import jax
import jax.numpy as jnp
import numpy as np
from jax import lax
from jax.experimental import pallas as pl
from jax.experimental.pallas import tpu as pltpu
from jax.sharding import PartitionSpec as P

TILE = 128
NY = 1024
NZ = 128
AMAX = 6
STEPS = 3
NREC = 512
SHOTS = 16
PLANES = 16
ROWS = AMAX * TILE
CHUNK = NY // SHOTS
MODES = 128
DEPTH = 2
SHIFTS = NY // TILE - AMAX + 1
DAMPING = 1.0
SIGMA_Z = 4.0
MESH = pl.DeviceIdType.MESH
HIGHEST = lax.Precision.HIGHEST
LAYERS = 8
SIDE = 4
PEN_REL = [(dy, dx) for dy in range(SIDE) for dx in range(SIDE) if (dy, dx) != (0, 0)]
SHOT_REL = [(dz, dc) for dz in range(LAYERS) for dc in range(2) if (dz, dc) != (0, 0)]


def wave_table(length, spread):
    half = MODES // 2
    order = np.concatenate([np.arange(half), np.arange(1, half + 1)])
    angle = 2.0 * np.pi * ((order[:, None] * np.arange(length)[None, :]) % length) / length
    waves = np.where(np.arange(2 * half)[:, None] < half, np.cos(angle), np.sin(angle))
    weights = np.exp(-0.5 * (spread * 2.0 * np.pi * order / length) ** 2) / length
    weights = np.where(order == 0, weights, 2.0 * weights)
    return waves.T, weights


def circulant_table(length, spread):
    frequency = np.fft.fftfreq(length)
    weights = np.exp(-0.5 * (spread * 2.0 * np.pi * frequency) ** 2)
    vector = np.real(np.fft.ifft(weights))
    position = np.arange(length)
    return vector[(position[:, None] - position[None, :]) % length].astype(np.float32)


def gauss_table(total, spread):
    position = np.arange(total)
    distance = (position[:, None] - position[None, :]).astype(np.float64)
    table = np.exp(-0.5 * (distance / spread) ** 2) / (spread * math.sqrt(2.0 * math.pi))
    return table.astype(np.float32)


def operator_table():
    waves, weights = wave_table(NY, float(NY) / float(SHOTS))
    z_part = circulant_table(NZ, SIGMA_Z)
    return np.concatenate([waves, z_part, np.tile(weights, (8, 1))]).astype(np.float32)


def block_rows(b, pad=0):
    return pl.ds(pl.multiple_of(b * TILE + pad, 8), TILE)


def kernel(
    aperture,
    source_cell,
    wavelet,
    gauss,
    courant_hbm,
    source_hbm,
    adjoint_hbm,
    strips_hbm,
    cells_hbm,
    residuals_hbm,
    table_hbm,
    precond_out,
    smooth_out,
    courant,
    source,
    adjoint,
    strips,
    cells,
    residuals,
    table,
    ua,
    ub,
    ra,
    rb,
    cw,
    hit,
    inj,
    from_low,
    from_high,
    grad,
    light,
    split_g,
    split_l,
    pair_g,
    pair_l,
    mine_g,
    mine_l,
    ring_g,
    ring_l,
    tiles,
    tiles_in,
    turned,
    coef,
    coef_in,
    total,
    load_sem,
    halo_send,
    halo_recv,
    pair_send,
    pair_recv,
    ring_send,
    ring_recv,
    tiles_send,
    tiles_recv,
    coef_send,
    coef_recv,
    total_send,
    total_recv,
):
    shot = lax.axis_index("shot")
    pen = lax.axis_index("pen")
    z, core = shot // 2, lax.rem(shot, 2)
    py, px = pen // SIDE, lax.rem(pen, SIDE)

    def pen_peer(rel):
        dy, dx = rel
        return (shot, lax.rem(py + dy, SIDE) * SIDE + lax.rem(px + dx, SIDE))

    def shot_peer(rel):
        dz, dc = rel
        return lax.rem(z + dz, LAYERS) * 2 + lax.rem(core + dc, 2)

    loads = []
    for i, (origin, place) in enumerate(
        (
            (source_hbm, source),
            (adjoint_hbm, adjoint),
            (courant_hbm, courant),
            (cells_hbm, cells),
            (residuals_hbm, residuals),
            (strips_hbm, strips),
            (table_hbm, table),
        )
    ):
        loads.append(pltpu.make_async_copy(origin, place, load_sem.at[i]))
        loads[i].start()

    barrier = pltpu.get_barrier_semaphore()
    for rel in PEN_REL:
        pl.semaphore_signal(barrier, inc=1, device_id=pen_peer(rel), device_id_type=MESH)
    for rel in SHOT_REL:
        pl.semaphore_signal(
            barrier, inc=1, device_id=(shot_peer(rel), pen), device_id_type=MESH
        )

    first = aperture[0, 0]
    count = aperture[0, 1]
    window = jnp.minimum(first, NY // TILE - AMAX)
    low = first - window
    high = low + count
    start = window * TILE

    edge = jnp.zeros((8, NZ), jnp.float32)
    for ref in (ua, ub, ra, rb):
        ref[pl.ds(0, 8), :] = edge
        ref[pl.ds(ROWS + 8, 8), :] = edge

    lane = lax.broadcasted_iota(jnp.int32, (TILE, NZ), 1)
    row = lax.broadcasted_iota(jnp.int32, (TILE, NZ), 0)

    def pick(options, like):
        where_from = like * 0 + window
        out = options[SHIFTS - 1]
        for i in range(SHIFTS - 2, -1, -1):
            out = jnp.where(where_from == i, options[i], out)
        return out

    def take_window(b, places):
        row_here = row + b * TILE
        inside = (row_here >= low * TILE) & (row_here < high * TILE)
        for ref, lead, out, pad in places:
            options = [ref[(*lead, block_rows(b, i * TILE))] for i in range(SHIFTS)]
            out[block_rows(b, pad), :] = jnp.where(inside, pick(options, row), 0.0)

    def load_block(places):
        def body(b, carry):
            take_window(b, places)
            return carry

        lax.fori_loop(0, AMAX, body, 0)

    loads[0].wait()
    load_block([(source, (0,), ua, 8)])

    pl.semaphore_wait(barrier, len(PEN_REL) + len(SHOT_REL))

    up = (shot, lax.rem(pen + 1, PLANES))
    down = (shot, lax.rem(pen + PLANES - 1, PLANES))

    def halo(state, slot):
        body = state.at[pl.ds(8, ROWS), :]
        upward = pltpu.make_async_remote_copy(
            body, from_low.at[slot], halo_send.at[slot, 0], halo_recv.at[slot, 0],
            device_id=up, device_id_type=MESH,
        )
        downward = pltpu.make_async_remote_copy(
            body, from_high.at[slot], halo_send.at[slot, 1], halo_recv.at[slot, 1],
            device_id=down, device_id_type=MESH,
        )

        class Pair:
            def start(self):
                pl.when(pen < PLANES - 1)(upward.start)
                pl.when(pen > 0)(downward.start)

            def sent(self):
                pl.when(pen < PLANES - 1)(upward.wait_send)
                pl.when(pen > 0)(downward.wait_send)

            def arrived(self):
                pl.when(pen > 0)(upward.wait_recv)
                pl.when(pen < PLANES - 1)(downward.wait_recv)

        return Pair()

    not_first = lane > 0
    not_last = lane < NZ - 1

    def laplace(state, slot, b):
        wide = state[pl.ds(pl.multiple_of(b * TILE, TILE), TILE + 16), :]
        here = wide[8 : TILE + 8]
        at = block_rows(b)
        beside = from_low[slot, at, :] + from_high[slot, at, :]
        beside = beside + pltpu.roll(wide, 1, 0)[8 : TILE + 8]
        beside = beside + pltpu.roll(wide, TILE + 15, 0)[8 : TILE + 8]
        beside = beside + jnp.where(not_first, pltpu.roll(here, 1, 1), 0.0)
        beside = beside + jnp.where(not_last, pltpu.roll(here, NZ - 1, 1), 0.0)
        return here, beside - 6.0 * here

    def source_step(now, old, slot, moment, adjoint_now, last):
        amplitude = wavelet[0, moment]

        def body(b, carry):
            here, lap = laplace(now, slot, b)
            at = block_rows(b)
            at8 = block_rows(b, 8)
            before = old[at8, :]
            new = 2.0 * here - before + cw[at, :] * (lap + amplitude * hit[at, :])
            row_here = row + b * TILE
            for i in range(2):
                new = jnp.where(
                    row_here == low * TILE + i, strips[moment, 0, pl.ds(i, 1), :], new
                )
                new = jnp.where(
                    row_here == high * TILE - 2 + i, strips[moment, 1, pl.ds(i, 1), :], new
                )
            at256 = block_rows(b, 2 * TILE)
            step = (before - 2.0 * here + new) * adjoint_now[at8, :]
            if moment == 0:
                grad[at256, :] = step
                light[at256, :] = here * here
            else:
                grad[at256, :] = grad[at256, :] + step
            if not last:
                old[at8, :] = new
            if moment < STEPS - 1 and moment > 0:
                light[at256, :] = light[at256, :] + here * here + new * new
            return carry

        lax.fori_loop(0, AMAX, body, 0)

    def adjoint_step(now, old, slot, moment):
        def body(b, carry):
            here, lap = laplace(now, slot, b)
            at = block_rows(b)
            at8 = block_rows(b, 8)
            old[at8, :] = 2.0 * here - old[at8, :] + cw[at, :] * (lap + inj[moment, at, :])
            return carry

        lax.fori_loop(0, AMAX, body, 0)

    u0, r0, u1, r1, u2 = halo(ua, 0), halo(ra, 1), halo(ub, 2), halo(rb, 3), halo(ua, 4)
    u0.start()
    load_block([(source, (1,), ub, 8)])

    @pl.when(pen == 0)
    def _():
        from_low[...] = jnp.zeros_like(from_low)

    @pl.when(pen == PLANES - 1)
    def _():
        from_high[...] = jnp.zeros_like(from_high)

    loads[1].wait()
    load_block([(adjoint, (0,), ra, 8), (adjoint, (1,), rb, 8)])
    for load in loads[2:]:
        load.wait()
    load_block([(courant, (), cw, 0)])

    cell_row = jnp.where(cells[pl.ds(0, 1), :] == pen, cells[pl.ds(1, 1), :] - start, -1)
    slab = lax.broadcasted_iota(jnp.int32, (2 * NZ, NREC), 0)
    values = jnp.where(
        slab == DEPTH,
        residuals[0],
        jnp.where(slab == NZ + DEPTH, residuals[1], 0.0),
    )
    fine = []
    for _ in range(3):
        piece = values.astype(jnp.bfloat16)
        values = values - piece.astype(jnp.float32)
        fine.append(piece)
    rows_wide = lax.broadcasted_iota(jnp.int32, (TILE, NREC), 0)

    def inject_block(b, carry):
        chosen = jnp.where(rows_wide == cell_row - b * TILE, 1.0, 0.0).astype(jnp.bfloat16)
        out = jnp.zeros((TILE, 2 * NZ), jnp.float32)
        for piece in fine:
            out = out + lax.dot_general(
                chosen, piece, (((1,), (1,)), ((), ())), preferred_element_type=jnp.float32
            )
        at = block_rows(b)
        inj[0, at, :] = out[:, :NZ]
        inj[1, at, :] = out[:, NZ:]
        key = row + (b * TILE + pen * NY)
        cell = source_cell[0, 0] * NY + source_cell[0, 1] - start
        here = (key == cell) & (lane == source_cell[0, 2])
        hit[at, :] = jnp.where(here, 1.0, 0.0)
        return carry

    lax.fori_loop(0, AMAX, inject_block, 0)
    for ref in (grad, light):
        ref[pl.ds(0, 2 * TILE), :] = jnp.zeros((2 * TILE, NZ), jnp.float32)
        ref[pl.ds(ROWS + 2 * TILE, 2 * TILE), :] = jnp.zeros((2 * TILE, NZ), jnp.float32)

    def spread(full, split):
        def body(g, carry):
            options = []
            for shift in range(SHIFTS):
                options.append(full[block_rows(g, (SHIFTS - 1 - shift) * TILE), :])
            flat = jnp.transpose(pick(options, row))
            columns = pl.ds(pl.multiple_of(g * TILE, TILE), TILE)
            for s in range(SHOTS):
                split[s % 2, s // 2, :, columns] = flat[8 * s : 8 * s + 8]
            return carry

        lax.fori_loop(0, NY // TILE, body, 0)

    def to_pair(split, pair, k):
        return pltpu.make_async_remote_copy(
            split.at[1 - core], pair, pair_send.at[k], pair_recv.at[k],
            device_id=(2 * z + 1 - core, pen), device_id_type=MESH,
        )

    def to_ring(split, pair, mine, ring, k):
        mine[...] = split[core] + pair[...]
        copies = []
        for d in range(1, LAYERS):
            target = lax.rem(z + d, LAYERS)
            copies.append(
                pltpu.make_async_remote_copy(
                    mine.at[target], ring.at[d - 1], ring_send.at[k, d - 1],
                    ring_recv.at[k, d - 1],
                    device_id=(2 * target + core, pen), device_id_type=MESH,
                )
            )
        return copies

    u0.sent()
    r0.start()
    u0.arrived()
    source_step(ua, ub, 0, 0, ra, False)
    r0.sent()
    u1.start()
    r0.arrived()
    adjoint_step(ra, rb, 1, 0)
    u1.sent()
    r1.start()
    u1.arrived()
    source_step(ub, ua, 2, 1, rb, False)
    spread(light, split_l)
    pair_light = to_pair(split_l, pair_l, 0)
    pair_light.start()
    r1.sent()
    u2.start()
    pair_light.wait()
    ring_light = to_ring(split_l, pair_l, mine_l, ring_l, 0)
    for copy in ring_light:
        copy.start()
    r1.arrived()
    adjoint_step(rb, ra, 3, 1)
    u2.arrived()
    source_step(ua, ub, 4, 2, ra, True)
    spread(grad, split_g)
    pair_grad = to_pair(split_g, pair_g, 1)
    pair_grad.start()
    for copy in ring_light:
        copy.wait()
    lighting = mine_l[z]
    for d in range(LAYERS - 1):
        lighting = lighting + ring_l[d]
    u2.sent()
    pair_grad.wait()
    ring_grad = to_ring(split_g, pair_g, mine_g, ring_g, 1)
    for copy in ring_grad:
        copy.start()
    for copy in ring_grad:
        copy.wait()
    gradient = mine_g[z]
    for d in range(LAYERS - 1):
        gradient = gradient + ring_g[d]
    precond = gradient / (lighting + DAMPING)
    for h in range(LAYERS):
        tiles[h] = precond[:, h * TILE : (h + 1) * TILE]
    tile_copies = []
    for i, rel in enumerate(SHOT_REL):
        peer = shot_peer(rel)
        tile_copies.append(
            pltpu.make_async_remote_copy(
                tiles.at[peer // 2], tiles_in.at[shot], tiles_send.at[i], tiles_recv.at[i],
                device_id=(peer, pen), device_id_type=MESH,
            )
        )
    tally = jnp.dot(
        precond, table[pl.ds(0, NY), :], precision=HIGHEST, preferred_element_type=jnp.float32
    )
    coef[...] = tally
    copies = []
    for i, rel in enumerate(PEN_REL):
        copies.append(
            pltpu.make_async_remote_copy(
                coef, coef_in.at[i], coef_send.at[i], coef_recv.at[i],
                device_id=pen_peer(rel), device_id_type=MESH,
            )
        )
    for copy in copies:
        copy.start()
    for copy in tile_copies:
        copy.start()
    tiles_in[shot] = tiles[z]
    mixed = tally * gauss[pen, pen]
    for copy in copies:
        copy.wait()
    for i, (dy, dx) in enumerate(PEN_REL):
        origin = lax.rem(py + SIDE - dy, SIDE) * SIDE + lax.rem(px + SIDE - dx, SIDE)
        mixed = mixed + coef_in[i] * gauss[pen, origin]
    total[shot] = mixed * table[pl.ds(NY + NZ, 8), :]
    copies = []
    for i, rel in enumerate(SHOT_REL):
        copies.append(
            pltpu.make_async_remote_copy(
                total.at[shot], total.at[shot], total_send.at[i], total_recv.at[i],
                device_id=(shot_peer(rel), pen), device_id_type=MESH,
            )
        )
    for copy in copies:
        copy.start()
    for copy in tile_copies:
        copy.wait()
    turned[...] = jnp.transpose(tiles_in[...].reshape(NZ, TILE))
    precond_out[...] = turned[pl.ds(pl.multiple_of(core * CHUNK, CHUNK), CHUNK), :]
    for copy in copies:
        copy.wait()
    wide = lax.dot_general(
        table[pl.ds(pl.multiple_of(shot * CHUNK, CHUNK), CHUNK), :],
        total[...].reshape(NZ, MODES),
        (((1,), (1,)), ((), ())),
        precision=HIGHEST,
        preferred_element_type=jnp.float32,
    )
    smooth_out[...] = jnp.dot(
        wide, table[pl.ds(NY, NZ), :], precision=HIGHEST, preferred_element_type=jnp.float32
    )


def on_device(
    courant,
    source_states,
    adjoint_states,
    strips,
    aperture,
    source_cell,
    wavelet,
    receiver_cells,
    residuals,
):
    table = operator_table()
    vmem = pl.BlockSpec(memory_space=pltpu.VMEM)
    hbm = pl.BlockSpec(memory_space=pltpu.HBM)
    smem = pl.BlockSpec(memory_space=pltpu.SMEM)
    f32 = jnp.float32
    dma = pltpu.SemaphoreType.DMA
    others = SHOTS - 1
    state = pltpu.VMEM((ROWS + 16, NZ), f32)
    field = pltpu.VMEM((ROWS, NZ), f32)
    precond, smooth = pl.pallas_call(
        kernel,
        out_shape=[jax.ShapeDtypeStruct((CHUNK, NZ), f32)] * 2,
        in_specs=[smem] * 4 + [hbm] * 7,
        out_specs=[vmem, vmem],
        scratch_shapes=[
            pltpu.VMEM((NY, NZ), f32),
            pltpu.VMEM((2, NY, NZ), f32),
            pltpu.VMEM((2, NY, NZ), f32),
            pltpu.VMEM((STEPS, 2, 2, NZ), f32),
            pltpu.VMEM((2, NREC), jnp.int32),
            pltpu.VMEM((STEPS, 1, NREC), f32),
            pltpu.VMEM(table.shape, f32),
            state,
            state,
            state,
            state,
            field,
            field,
            pltpu.VMEM((2, ROWS, NZ), f32),
            pltpu.VMEM((5, ROWS, NZ), f32),
            pltpu.VMEM((5, ROWS, NZ), f32),
            pltpu.VMEM((ROWS + 4 * TILE, NZ), f32),
            pltpu.VMEM((ROWS + 4 * TILE, NZ), f32),
            pltpu.VMEM((2, LAYERS, 8, NY), f32),
            pltpu.VMEM((2, LAYERS, 8, NY), f32),
            pltpu.VMEM((LAYERS, 8, NY), f32),
            pltpu.VMEM((LAYERS, 8, NY), f32),
            pltpu.VMEM((LAYERS, 8, NY), f32),
            pltpu.VMEM((LAYERS, 8, NY), f32),
            pltpu.VMEM((LAYERS - 1, 8, NY), f32),
            pltpu.VMEM((LAYERS - 1, 8, NY), f32),
            pltpu.VMEM((LAYERS, 8, TILE), f32),
            pltpu.VMEM((SHOTS, 8, TILE), f32),
            pltpu.VMEM((TILE, NZ), f32),
            pltpu.VMEM((8, NZ), f32),
            pltpu.VMEM((others, 8, NZ), f32),
            pltpu.VMEM((SHOTS, 8, NZ), f32),
            dma((7,)),
            dma((5, 2)),
            dma((5, 2)),
            dma((2,)),
            dma((2,)),
            dma((2, LAYERS - 1)),
            dma((2, LAYERS - 1)),
            dma((others,)),
            dma((others,)),
            dma((others,)),
            dma((others,)),
            dma((others,)),
            dma((others,)),
        ],
        compiler_params=pltpu.CompilerParams(
            collective_id=0, has_side_effects=True, vmem_limit_bytes=48 << 20
        ),
        name="inversion",
    )(
        aperture,
        source_cell,
        wavelet,
        jnp.asarray(gauss_table(PLANES, float(PLANES) / 4.0)),
        courant[0],
        source_states[0, :, 0],
        adjoint_states[0, :, 0],
        strips[0, :, :, 0],
        receiver_cells[0].T,
        residuals.transpose(1, 0, 2),
        jnp.asarray(table),
    )
    return (precond[None], smooth[None])


def solution(mesh):
    placed = (
        P("pen", None, None),
        P("shot", None, "pen", None, None),
        P("shot", None, "pen", None, None),
        P("shot", None, None, "pen", None, None),
        P("shot", None),
        P("shot", None),
        P("shot", None),
        P("shot", None, None),
        P("shot", None, None),
    )
    return jax.shard_map(
        on_device,
        mesh=mesh,
        in_specs=placed,
        out_specs=(P("pen", "shot", None), P("pen", "shot", None)),
        check_vma=False,
    )
```

```python
import math

import jax
import jax.numpy as jnp
import numpy as np
from jax import lax
from jax.experimental import pallas as pl
from jax.experimental.pallas import tpu as pltpu
from jax.sharding import PartitionSpec as P

TILE = 128
NY = 1024
NZ = 128
AMAX = 6
STEPS = 3
NREC = 512
SHOTS = 16
PLANES = 16
ROWS = AMAX * TILE
CHUNK = NY // SHOTS
MODES = 128
DEPTH = 2
SHIFTS = NY // TILE - AMAX + 1
QUARTERS = 4
DEEP = NZ // QUARTERS
DAMPING = 1.0
SIGMA_Z = 4.0
MESH = pl.DeviceIdType.MESH
HIGHEST = lax.Precision.HIGHEST
LAYERS = 8
SIDE = 4
PEN_REL = [(dy, dx) for dy in range(SIDE) for dx in range(SIDE) if (dy, dx) != (0, 0)]
SHOT_REL = [(dz, dc) for dz in range(LAYERS) for dc in range(2) if (dz, dc) != (0, 0)]


def wave_table(length, spread):
    half = MODES // 2
    order = np.concatenate([np.arange(half), np.arange(1, half + 1)])
    angle = 2.0 * np.pi * ((order[:, None] * np.arange(length)[None, :]) % length) / length
    waves = np.where(np.arange(2 * half)[:, None] < half, np.cos(angle), np.sin(angle))
    weights = np.exp(-0.5 * (spread * 2.0 * np.pi * order / length) ** 2) / length
    weights = np.where(order == 0, weights, 2.0 * weights)
    return waves.T, weights


def circulant_table(length, spread):
    frequency = np.fft.fftfreq(length)
    weights = np.exp(-0.5 * (spread * 2.0 * np.pi * frequency) ** 2)
    vector = np.real(np.fft.ifft(weights))
    position = np.arange(length)
    return vector[(position[:, None] - position[None, :]) % length].astype(np.float32)


def gauss_table(total, spread):
    position = np.arange(total)
    distance = (position[:, None] - position[None, :]).astype(np.float64)
    table = np.exp(-0.5 * (distance / spread) ** 2) / (spread * math.sqrt(2.0 * math.pi))
    return table.astype(np.float32)


def operator_table():
    waves, weights = wave_table(NY, float(NY) / float(SHOTS))
    z_part = circulant_table(NZ, SIGMA_Z)
    return np.concatenate([waves, z_part, np.tile(weights, (8, 1))]).astype(np.float32)


def block_rows(b, pad=0):
    return pl.ds(pl.multiple_of(b * TILE + pad, 8), TILE)


def kernel(
    aperture,
    source_cell,
    wavelet,
    gauss,
    courant_hbm,
    source_hbm,
    adjoint_hbm,
    strips_hbm,
    cells_hbm,
    residuals_hbm,
    table_hbm,
    precond_out,
    smooth_out,
    courant,
    source,
    adjoint,
    strips,
    cells,
    residuals,
    table,
    ua,
    ub,
    ra,
    rb,
    cw,
    hit,
    inj,
    from_low,
    from_high,
    grad,
    light,
    turned_u,
    low_turned,
    high_turned,
    slope,
    whole,
    split_g,
    split_l,
    pair_g,
    pair_l,
    mine_g,
    mine_l,
    ring_g,
    ring_l,
    tiles,
    tiles_in,
    turned,
    coef,
    coef_in,
    total,
    known,
    load_sem,
    last_send,
    last_recv,
    halo_send,
    halo_recv,
    pair_send,
    pair_recv,
    ring_send,
    ring_recv,
    tiles_send,
    tiles_recv,
    coef_send,
    coef_recv,
    total_send,
    total_recv,
):
    shot = lax.axis_index("shot")
    pen = lax.axis_index("pen")
    z, core = shot // 2, lax.rem(shot, 2)
    py, px = pen // SIDE, lax.rem(pen, SIDE)

    def pen_peer(rel):
        dy, dx = rel
        return (shot, lax.rem(py + dy, SIDE) * SIDE + lax.rem(px + dx, SIDE))

    def shot_peer(rel):
        dz, dc = rel
        return lax.rem(z + dz, LAYERS) * 2 + lax.rem(core + dc, 2)

    loads = []
    for i, (origin, place) in enumerate(
        (
            (source_hbm, source),
            (adjoint_hbm, adjoint),
            (courant_hbm, courant),
            (cells_hbm, cells),
            (residuals_hbm, residuals),
            (strips_hbm, strips),
            (table_hbm, table),
        )
    ):
        loads.append(pltpu.make_async_copy(origin, place, load_sem.at[i]))
        loads[i].start()

    barrier = pltpu.get_barrier_semaphore()
    def pen_at(offset):
        return (shot, lax.rem(pen + offset, PLANES))

    def shot_at(dz, dc):
        return (lax.rem(z + dz, LAYERS) * 2 + lax.rem(core + dc, 2), pen)

    near_pen = [pen_at(o) for o in (1, PLANES - 1, SIDE, PLANES - SIDE)]
    near_shot = [shot_at(1, 0), shot_at(LAYERS - 1, 0), shot_at(0, 1)]
    for peer in near_pen + near_shot:
        pl.semaphore_signal(barrier, inc=1, device_id=peer, device_id_type=MESH)

    greetings = [
        (0, near_pen),
        (1, near_shot),
        (2, [pen_at(SIDE), pen_at(PLANES - SIDE)]),
        (3, [shot_at(2, 0), shot_at(LAYERS - 2, 0)]),
        (4, [shot_at(0, 1)]),
    ]

    def greet(k):
        for peer in greetings[k][1]:
            pl.semaphore_signal(known.at[k], inc=1, device_id=peer, device_id_type=MESH)

    def greeted(k):
        pl.semaphore_wait(known.at[k], len(greetings[k][1]))

    first = aperture[0, 0]
    count = aperture[0, 1]
    window = jnp.minimum(first, NY // TILE - AMAX)
    low = first - window
    high = low + count
    start = window * TILE

    edge = jnp.zeros((8, NZ), jnp.float32)
    for ref in (ua, ub, ra, rb):
        ref[pl.ds(0, 8), :] = edge
        ref[pl.ds(ROWS + 8, 8), :] = edge

    lane = lax.broadcasted_iota(jnp.int32, (TILE, NZ), 1)
    row = lax.broadcasted_iota(jnp.int32, (TILE, NZ), 0)

    def pick(options, like):
        where_from = like * 0 + window
        out = options[SHIFTS - 1]
        for i in range(SHIFTS - 2, -1, -1):
            out = jnp.where(where_from == i, options[i], out)
        return out

    def take_window(b, places):
        row_here = row + b * TILE
        inside = (row_here >= low * TILE) & (row_here < high * TILE)
        for ref, lead, out, pad in places:
            options = [ref[(*lead, block_rows(b, i * TILE))] for i in range(SHIFTS)]
            out[block_rows(b, pad), :] = jnp.where(inside, pick(options, row), 0.0)

    def load_block(places):
        def body(b, carry):
            take_window(b, places)
            return carry

        lax.fori_loop(0, AMAX, body, 0)

    loads[0].wait()
    load_block([(source, (0,), ua, 8)])

    pl.semaphore_wait(barrier, len(near_pen) + len(near_shot))

    up, down = near_pen[0], near_pen[1]

    def exchange(body, low, high, send, recv):
        upward = pltpu.make_async_remote_copy(
            body, low, send.at[0], recv.at[0], device_id=up, device_id_type=MESH
        )
        downward = pltpu.make_async_remote_copy(
            body, high, send.at[1], recv.at[1], device_id=down, device_id_type=MESH
        )

        class Pair:
            def start(self):
                pl.when(pen < PLANES - 1)(upward.start)
                pl.when(pen > 0)(downward.start)

            def sent(self):
                pl.when(pen < PLANES - 1)(upward.wait_send)
                pl.when(pen > 0)(downward.wait_send)

            def arrived(self):
                pl.when(pen > 0)(upward.wait_recv)
                pl.when(pen < PLANES - 1)(downward.wait_recv)

        return Pair()

    def halo(state, slot):
        return exchange(
            state.at[pl.ds(8, ROWS), :],
            from_low.at[slot],
            from_high.at[slot],
            halo_send.at[slot],
            halo_recv.at[slot],
        )

    def halo_turned(k):
        at = pl.ds(k * DEEP, DEEP)
        return exchange(
            turned_u.at[at, :],
            low_turned.at[at, :],
            high_turned.at[at, :],
            last_send.at[k],
            last_recv.at[k],
        )

    not_first = lane > 0
    not_last = lane < NZ - 1

    def laplace(state, slot, b):
        wide = state[pl.ds(pl.multiple_of(b * TILE, TILE), TILE + 16), :]
        here = wide[8 : TILE + 8]
        at = block_rows(b)
        beside = pltpu.roll(wide, 1, 0)[8 : TILE + 8]
        beside = beside + pltpu.roll(wide, TILE + 15, 0)[8 : TILE + 8]
        beside = beside + jnp.where(not_first, pltpu.roll(here, 1, 1), 0.0)
        beside = beside + jnp.where(not_last, pltpu.roll(here, NZ - 1, 1), 0.0)
        if slot is not None:
            beside = beside + (from_low[slot, at, :] + from_high[slot, at, :])
        return here, beside - 6.0 * here

    def with_strips(b, moment, new):
        row_here = row + b * TILE
        for i in range(2):
            new = jnp.where(
                row_here == low * TILE + i, strips[moment, 0, pl.ds(i, 1), :], new
            )
            new = jnp.where(
                row_here == high * TILE - 2 + i, strips[moment, 1, pl.ds(i, 1), :], new
            )
        return new

    def columns(b, pad=0):
        return pl.ds(pl.multiple_of(b * TILE + pad, TILE), TILE)

    def source_step(now, old, slot, moment, adjoint_now):
        amplitude = wavelet[0, moment]

        def body(b, carry):
            here, lap = laplace(now, slot, b)
            at = block_rows(b)
            at8 = block_rows(b, 8)
            before = old[at8, :]
            new = 2.0 * here - before + cw[at, :] * (lap + amplitude * hit[at, :])
            new = with_strips(b, moment, new)
            at256 = block_rows(b, 2 * TILE)
            step = (before - 2.0 * here + new) * adjoint_now[at8, :]
            old[at8, :] = new
            if moment == 0:
                grad[at, :] = step
                light[at256, :] = here * here
            else:
                grad[at, :] = grad[at, :] + step
                light[at256, :] = light[at256, :] + here * here + new * new
                turned_u[:, columns(b)] = jnp.transpose(new)
            return carry

        lax.fori_loop(0, AMAX, body, 0)

    def last_step(now, old, moment, adjoint_now):
        amplitude = wavelet[0, moment]

        def body(b, carry):
            here, lap = laplace(now, None, b)
            at = block_rows(b)
            at8 = block_rows(b, 8)
            before = old[at8, :]
            new = 2.0 * here - before + cw[at, :] * (lap + amplitude * hit[at, :])
            new = with_strips(b, moment, new)
            free = cw[at, :]
            row_here = row + b * TILE
            for i in range(2):
                free = jnp.where(row_here == low * TILE + i, 0.0, free)
                free = jnp.where(row_here == high * TILE - 2 + i, 0.0, free)
            ahead = adjoint_now[at8, :]
            known_part = grad[at, :] + (before - 2.0 * here + new) * ahead
            whole[:, columns(b, 2 * TILE)] = jnp.transpose(known_part)
            slope[:, columns(b)] = jnp.transpose(free * ahead)
            return carry

        lax.fori_loop(0, AMAX, body, 0)

    def adjoint_step(now, old, slot, moment):
        def body(b, carry):
            here, lap = laplace(now, slot, b)
            at = block_rows(b)
            at8 = block_rows(b, 8)
            old[at8, :] = 2.0 * here - old[at8, :] + cw[at, :] * (lap + inj[moment, at, :])
            return carry

        lax.fori_loop(0, AMAX, body, 0)

    u0, r0, u1, r1 = halo(ua, 0), halo(ra, 1), halo(ub, 2), halo(rb, 3)
    u2 = [halo_turned(k) for k in range(QUARTERS)]
    u0.start()
    greet(0)
    greet(1)
    load_block([(source, (1,), ub, 8)])

    @pl.when(pen == 0)
    def _():
        from_low[...] = jnp.zeros_like(from_low)
        low_turned[...] = jnp.zeros_like(low_turned)

    @pl.when(pen == PLANES - 1)
    def _():
        from_high[...] = jnp.zeros_like(from_high)
        high_turned[...] = jnp.zeros_like(high_turned)

    loads[1].wait()
    load_block([(adjoint, (0,), ra, 8), (adjoint, (1,), rb, 8)])
    u0.sent()
    r0.start()
    for load in loads[2:]:
        load.wait()
    greeted(0)
    greeted(1)
    greet(2)
    greet(3)
    load_block([(courant, (), cw, 0)])

    cell_row = jnp.where(cells[pl.ds(0, 1), :] == pen, cells[pl.ds(1, 1), :] - start, -1)
    slab = lax.broadcasted_iota(jnp.int32, (8, NREC), 0)
    values = jnp.where(lax.rem(slab, 2) == 0, residuals[0], residuals[1])
    coarse = values.astype(jnp.bfloat16).astype(jnp.float32)
    middle = (values - coarse).astype(jnp.bfloat16).astype(jnp.float32)
    fine = values - coarse - middle
    values = jnp.where(slab < DEPTH + 2, coarse, jnp.where(slab < DEPTH + 4, middle, fine))
    values = jnp.where(slab < DEPTH, 0.0, values)
    values = jnp.concatenate([values, jnp.zeros((NZ - 8, NREC), jnp.float32)], axis=0)
    values = jnp.transpose(values).astype(jnp.bfloat16)
    rows_wide = lax.broadcasted_iota(jnp.int32, (TILE, NREC), 0)

    def inject_block(b, carry):
        chosen = jnp.where(rows_wide == cell_row - b * TILE, 1.0, 0.0).astype(jnp.bfloat16)
        out = jnp.dot(chosen, values, preferred_element_type=jnp.float32)
        out = out + pltpu.roll(out, NZ - 2, 1) + pltpu.roll(out, NZ - 4, 1)
        at = block_rows(b)
        inj[0, at, :] = jnp.where(lane == DEPTH, out, 0.0)
        inj[1, at, :] = jnp.where(lane == DEPTH, pltpu.roll(out, NZ - 1, 1), 0.0)
        key = row + (b * TILE + pen * NY)
        cell = source_cell[0, 0] * NY + source_cell[0, 1] - start
        here = (key == cell) & (lane == source_cell[0, 2])
        hit[at, :] = jnp.where(here, 1.0, 0.0)
        return carry

    lax.fori_loop(0, AMAX, inject_block, 0)
    light[pl.ds(0, 2 * TILE), :] = jnp.zeros((2 * TILE, NZ), jnp.float32)
    light[pl.ds(ROWS + 2 * TILE, 2 * TILE), :] = jnp.zeros((2 * TILE, NZ), jnp.float32)
    whole[:, pl.ds(0, 2 * TILE)] = jnp.zeros((NZ, 2 * TILE), jnp.float32)
    whole[:, pl.ds(ROWS + 2 * TILE, 2 * TILE)] = jnp.zeros((NZ, 2 * TILE), jnp.float32)
    greeted(2)
    greeted(3)
    greet(4)

    def spread_light():
        def body(g, carry):
            options = []
            for shift in range(SHIFTS):
                options.append(light[block_rows(g, (SHIFTS - 1 - shift) * TILE), :])
            flat = jnp.transpose(pick(options, row))
            for d in range(SHOTS):
                k, j = d // 4, d % 4
                split_l[j % 2, k, j // 2, :, columns(g)] = flat[8 * d : 8 * d + 8]
            return carry

        lax.fori_loop(0, NY // TILE, body, 0)

    def spread_quarter(k):
        at = pl.ds(k * DEEP, DEEP)
        inner = pl.ds(2 * TILE, ROWS)
        pushed = low_turned[at, :] + high_turned[at, :]
        whole[at, inner] = whole[at, inner] + slope[at, :] * pushed
        for j in range(4):
            rows8 = pl.ds(k * DEEP + 8 * j, 8)
            options = []
            for shift in range(SHIFTS):
                options.append(whole[rows8, pl.ds((SHIFTS - 1 - shift) * TILE, NY)])
            like = lax.broadcasted_iota(jnp.int32, (8, NY), 0)
            split_g[j % 2, k, j // 2] = pick(options, like)

    class Sum:
        def __init__(self, split, pair, mine, ring, which):
            self.split, self.pair, self.mine, self.ring = split, pair, mine, ring
            self.pairs, self.targets = [], []
            for k in range(QUARTERS):
                self.pairs.append(
                    pltpu.make_async_remote_copy(
                        split.at[1 - core, k], pair.at[k], pair_send.at[which, k],
                        pair_recv.at[which, k],
                        device_id=shot_at(0, 1), device_id_type=MESH,
                    )
                )
                for h in range(2):
                    target = k + 4 * h
                    slot = lax.rem(target - z + 2 * LAYERS - 1, LAYERS)
                    self.targets.append(
                        pltpu.make_async_remote_copy(
                            mine.at[k, h], ring.at[slot], ring_send.at[which, target],
                            ring_recv.at[which, slot],
                            device_id=(2 * target + core, pen), device_id_type=MESH,
                        )
                    )
            self.arrivals = [
                pltpu.make_async_remote_copy(
                    mine.at[0, 0], ring.at[slot], ring_send.at[which, 0],
                    ring_recv.at[which, slot],
                    device_id=shot_at(1, 0), device_id_type=MESH,
                )
                for slot in range(LAYERS - 1)
            ]

        def start_ring(self, k):
            self.pairs[k].wait()
            self.mine[k] = self.split[core, k] + self.pair[k]
            for h in range(2):
                pl.when(z != k + 4 * h)(self.targets[2 * k + h].start)

        def finish(self):
            total_here = self.mine[lax.rem(z, 4), z // 4]
            for slot in range(LAYERS - 1):
                self.arrivals[slot].wait_recv()
                total_here = total_here + self.ring[slot]
            for k in range(QUARTERS):
                for h in range(2):
                    pl.when(z != k + 4 * h)(self.targets[2 * k + h].wait_send)
            return total_here

    sum_l = Sum(split_l, pair_l, mine_l, ring_l, 0)
    sum_g = Sum(split_g, pair_g, mine_g, ring_g, 1)

    u0.arrived()
    source_step(ua, ub, 0, 0, ra)
    r0.sent()
    u1.start()
    greeted(4)
    r0.arrived()
    adjoint_step(ra, rb, 1, 0)
    u1.sent()
    r1.start()
    u1.arrived()
    source_step(ub, ua, 2, 1, rb)
    spread_light()
    for k in range(QUARTERS):
        sum_l.pairs[k].start()
    for k in range(QUARTERS):
        sum_l.start_ring(k)
    r1.sent()
    u2[0].start()
    u2[1].start()
    r1.arrived()
    adjoint_step(rb, ra, 3, 1)
    u2[0].sent()
    u2[2].start()
    last_step(ua, ub, 2, ra)
    u2[1].sent()
    u2[3].start()
    for k in range(QUARTERS):
        u2[k].arrived()
        spread_quarter(k)
        sum_g.pairs[k].start()
        if k > 0:
            sum_g.start_ring(k - 1)
    sum_g.start_ring(QUARTERS - 1)
    for k in range(2, QUARTERS):
        u2[k].sent()
    lighting = sum_l.finish()
    gradient = sum_g.finish()
    precond = gradient / (lighting + DAMPING)
    depth = 4 * lax.rem(z, 4) + 2 * (z // 4) + core
    for h in range(LAYERS):
        tiles[h] = precond[:, h * TILE : (h + 1) * TILE]
    tile_copies = []
    for i, rel in enumerate(SHOT_REL):
        peer = shot_peer(rel)
        tile_copies.append(
            pltpu.make_async_remote_copy(
                tiles.at[peer // 2], tiles_in.at[depth], tiles_send.at[i], tiles_recv.at[i],
                device_id=(peer, pen), device_id_type=MESH,
            )
        )
    tally = jnp.dot(
        precond, table[pl.ds(0, NY), :], precision=HIGHEST, preferred_element_type=jnp.float32
    )
    coef[...] = tally
    copies = []
    for i, rel in enumerate(PEN_REL):
        copies.append(
            pltpu.make_async_remote_copy(
                coef, coef_in.at[i], coef_send.at[i], coef_recv.at[i],
                device_id=pen_peer(rel), device_id_type=MESH,
            )
        )
    for copy in copies:
        copy.start()
    for copy in tile_copies:
        copy.start()
    tiles_in[depth] = tiles[z]
    mixed = tally * gauss[pen, pen]
    for copy in copies:
        copy.wait()
    for i, (dy, dx) in enumerate(PEN_REL):
        origin = lax.rem(py + SIDE - dy, SIDE) * SIDE + lax.rem(px + SIDE - dx, SIDE)
        mixed = mixed + coef_in[i] * gauss[pen, origin]
    total[depth] = mixed * table[pl.ds(NY + NZ, 8), :]
    copies = []
    for i, rel in enumerate(SHOT_REL):
        copies.append(
            pltpu.make_async_remote_copy(
                total.at[depth], total.at[depth], total_send.at[i], total_recv.at[i],
                device_id=(shot_peer(rel), pen), device_id_type=MESH,
            )
        )
    for copy in copies:
        copy.start()
    for copy in tile_copies:
        copy.wait()
    turned[...] = jnp.transpose(tiles_in[...].reshape(NZ, TILE))
    precond_out[...] = turned[pl.ds(pl.multiple_of(core * CHUNK, CHUNK), CHUNK), :]
    for copy in copies:
        copy.wait()
    wide = lax.dot_general(
        table[pl.ds(pl.multiple_of(shot * CHUNK, CHUNK), CHUNK), :],
        total[...].reshape(NZ, MODES),
        (((1,), (1,)), ((), ())),
        precision=HIGHEST,
        preferred_element_type=jnp.float32,
    )
    smooth_out[...] = jnp.dot(
        wide, table[pl.ds(NY, NZ), :], precision=HIGHEST, preferred_element_type=jnp.float32
    )


def on_device(
    courant,
    source_states,
    adjoint_states,
    strips,
    aperture,
    source_cell,
    wavelet,
    receiver_cells,
    residuals,
):
    table = operator_table()
    vmem = pl.BlockSpec(memory_space=pltpu.VMEM)
    hbm = pl.BlockSpec(memory_space=pltpu.HBM)
    smem = pl.BlockSpec(memory_space=pltpu.SMEM)
    f32 = jnp.float32
    dma = pltpu.SemaphoreType.DMA
    others = SHOTS - 1
    state = pltpu.VMEM((ROWS + 16, NZ), f32)
    field = pltpu.VMEM((ROWS, NZ), f32)
    precond, smooth = pl.pallas_call(
        kernel,
        out_shape=[jax.ShapeDtypeStruct((CHUNK, NZ), f32)] * 2,
        in_specs=[smem] * 4 + [hbm] * 7,
        out_specs=[vmem, vmem],
        scratch_shapes=[
            pltpu.VMEM((NY, NZ), f32),
            pltpu.VMEM((2, NY, NZ), f32),
            pltpu.VMEM((2, NY, NZ), f32),
            pltpu.VMEM((STEPS, 2, 2, NZ), f32),
            pltpu.VMEM((2, NREC), jnp.int32),
            pltpu.VMEM((STEPS, 1, NREC), f32),
            pltpu.VMEM(table.shape, f32),
            state,
            state,
            state,
            state,
            field,
            field,
            pltpu.VMEM((2, ROWS, NZ), f32),
            pltpu.VMEM((4, ROWS, NZ), f32),
            pltpu.VMEM((4, ROWS, NZ), f32),
            field,
            pltpu.VMEM((ROWS + 4 * TILE, NZ), f32),
            pltpu.VMEM((NZ, ROWS), f32),
            pltpu.VMEM((NZ, ROWS), f32),
            pltpu.VMEM((NZ, ROWS), f32),
            pltpu.VMEM((NZ, ROWS), f32),
            pltpu.VMEM((NZ, ROWS + 4 * TILE), f32),
            pltpu.VMEM((2, QUARTERS, 2, 8, NY), f32),
            pltpu.VMEM((2, QUARTERS, 2, 8, NY), f32),
            pltpu.VMEM((QUARTERS, 2, 8, NY), f32),
            pltpu.VMEM((QUARTERS, 2, 8, NY), f32),
            pltpu.VMEM((QUARTERS, 2, 8, NY), f32),
            pltpu.VMEM((QUARTERS, 2, 8, NY), f32),
            pltpu.VMEM((LAYERS, 8, NY), f32),
            pltpu.VMEM((LAYERS, 8, NY), f32),
            pltpu.VMEM((LAYERS, 8, TILE), f32),
            pltpu.VMEM((SHOTS, 8, TILE), f32),
            pltpu.VMEM((TILE, NZ), f32),
            pltpu.VMEM((8, NZ), f32),
            pltpu.VMEM((others, 8, NZ), f32),
            pltpu.VMEM((SHOTS, 8, NZ), f32),
            pltpu.SemaphoreType.REGULAR((5,)),
            dma((7,)),
            dma((QUARTERS, 2)),
            dma((QUARTERS, 2)),
            dma((4, 2)),
            dma((4, 2)),
            dma((2, QUARTERS)),
            dma((2, QUARTERS)),
            dma((2, LAYERS)),
            dma((2, LAYERS)),
            dma((others,)),
            dma((others,)),
            dma((others,)),
            dma((others,)),
            dma((others,)),
            dma((others,)),
        ],
        compiler_params=pltpu.CompilerParams(
            collective_id=0, has_side_effects=True, vmem_limit_bytes=63 << 20
        ),
        name="inversion",
    )(
        aperture,
        source_cell,
        wavelet,
        jnp.asarray(gauss_table(PLANES, float(PLANES) / 4.0)),
        courant[0],
        source_states[0, :, 0],
        adjoint_states[0, :, 0],
        strips[0, :, :, 0],
        receiver_cells[0].T,
        residuals.transpose(1, 0, 2),
        jnp.asarray(table),
    )
    return (precond[None], smooth[None])


def solution(mesh):
    placed = (
        P("pen", None, None),
        P("shot", None, "pen", None, None),
        P("shot", None, "pen", None, None),
        P("shot", None, None, "pen", None, None),
        P("shot", None),
        P("shot", None),
        P("shot", None),
        P("shot", None, None),
        P("shot", None, None),
    )
    return jax.shard_map(
        on_device,
        mesh=mesh,
        in_specs=placed,
        out_specs=(P("pen", "shot", None), P("pen", "shot", None)),
        check_vma=False,
    )
```

```python
import math

import jax
import jax.numpy as jnp
import numpy as np
from jax import lax
from jax.experimental import pallas as pl
from jax.experimental.pallas import tpu as pltpu
from jax.sharding import PartitionSpec as P

TILE = 128
NY = 1024
NZ = 128
AMAX = 6
STEPS = 3
NREC = 512
SHOTS = 16
PLANES = 16
ROWS = AMAX * TILE
CHUNK = NY // SHOTS
MODES = 128
DEPTH = 2
SHIFTS = NY // TILE - AMAX + 1
QUARTERS = 4
DEEP = NZ // QUARTERS
DAMPING = 1.0
SIGMA_Z = 4.0
MESH = pl.DeviceIdType.MESH
HIGHEST = lax.Precision.HIGHEST
LAYERS = 8
SIDE = 4


def hops(*steps):
    return -sum(min(step, size - step) for step, size in steps)


PEN_REL = sorted(
    [(dy, dx) for dy in range(SIDE) for dx in range(SIDE) if (dy, dx) != (0, 0)],
    key=lambda rel: hops((rel[0], SIDE), (rel[1], SIDE)),
)

SHOT_REL = sorted(
    [(dz, dc) for dz in range(LAYERS) for dc in range(2) if (dz, dc) != (0, 0)],
    key=lambda rel: hops((rel[0], LAYERS), (rel[1], 2)),
)


def wave_table(length, spread):
    half = MODES // 2
    order = np.concatenate([np.arange(half), np.arange(1, half + 1)])
    angle = 2.0 * np.pi * ((order[:, None] * np.arange(length)[None, :]) % length) / length
    waves = np.where(np.arange(2 * half)[:, None] < half, np.cos(angle), np.sin(angle))
    weights = np.exp(-0.5 * (spread * 2.0 * np.pi * order / length) ** 2) / length
    weights = np.where(order == 0, weights, 2.0 * weights)
    return waves.T, weights


def circulant_table(length, spread):
    frequency = np.fft.fftfreq(length)
    weights = np.exp(-0.5 * (spread * 2.0 * np.pi * frequency) ** 2)
    vector = np.real(np.fft.ifft(weights))
    position = np.arange(length)
    return vector[(position[:, None] - position[None, :]) % length].astype(np.float32)


def gauss_table(total, spread):
    position = np.arange(total)
    distance = (position[:, None] - position[None, :]).astype(np.float64)
    table = np.exp(-0.5 * (distance / spread) ** 2) / (spread * math.sqrt(2.0 * math.pi))
    return table.astype(np.float32)


def depth_slot(layer, core):
    return 4 * (layer % 4) + 2 * (layer // 4) + core


def operator_table():
    waves, weights = wave_table(NY, float(NY) / float(SHOTS))
    owners = [(core, layer) for core in range(2) for layer in range(LAYERS)]
    depths = [8 * depth_slot(layer, core) + i for core, layer in owners for i in range(8)]
    z_part = circulant_table(NZ, SIGMA_Z)[np.array(depths)]
    return np.concatenate([waves, z_part, np.tile(weights, (8, 1))]).astype(np.float32)


def cut_in_two(value):
    coarse = value.astype(jnp.bfloat16)
    return coarse, (value - coarse.astype(jnp.float32)).astype(jnp.bfloat16)


def four_sums(out, rows):
    first = out[:rows, :NZ] + (out[:rows, NZ:] + out[rows:, :NZ])
    return first + out[rows:, NZ:]


def block_rows(b, pad=0):
    return pl.ds(pl.multiple_of(b * TILE + pad, 8), TILE)


def kernel(
    aperture,
    source_cell,
    wavelet,
    gauss,
    courant_hbm,
    source_hbm,
    adjoint_hbm,
    strips_hbm,
    cells_hbm,
    residuals_hbm,
    table_hbm,
    both_out,
    courant,
    source,
    adjoint,
    strips,
    cells,
    residuals,
    table,
    ua,
    ub,
    ra,
    rb,
    cw,
    hit,
    inj,
    from_low,
    from_high,
    grad,
    light,
    turned_u,
    low_turned,
    high_turned,
    slope,
    whole,
    split_g,
    split_l,
    pair_g,
    pair_l,
    mine_g,
    mine_l,
    ring_g,
    ring_l,
    tiles,
    tiles_in,
    turned,
    coef,
    coef_in,
    total,
    waves_cut,
    mine_cut,
    z_cut,
    known,
    load_sem,
    last_send,
    last_recv,
    halo_send,
    halo_recv,
    pair_send,
    pair_recv,
    ring_send,
    ring_recv,
    tiles_send,
    tiles_recv,
    coef_send,
    coef_recv,
    total_send,
    total_recv,
):
    shot = lax.axis_index("shot")
    pen = lax.axis_index("pen")
    z, core = shot // 2, lax.rem(shot, 2)
    py, px = pen // SIDE, lax.rem(pen, SIDE)

    def pen_peer(rel):
        dy, dx = rel
        return (shot, lax.rem(py + dy, SIDE) * SIDE + lax.rem(px + dx, SIDE))

    loads = []
    for i, (origin, place) in enumerate(
        (
            (source_hbm.at[0], source.at[0]),
            (source_hbm.at[1], source.at[1]),
            (adjoint_hbm, adjoint),
            (courant_hbm, courant),
            (cells_hbm, cells),
            (residuals_hbm, residuals),
            (strips_hbm, strips),
            (table_hbm, table),
        )
    ):
        loads.append(pltpu.make_async_copy(origin, place, load_sem.at[i]))
    loads[0].start()

    barrier = pltpu.get_barrier_semaphore()
    def pen_at(offset):
        return (shot, lax.rem(pen + offset, PLANES))

    def shot_at(dz, dc):
        return (lax.rem(z + dz, LAYERS) * 2 + lax.rem(core + dc, 2), pen)

    near_pen = [pen_at(o) for o in (1, PLANES - 1, SIDE, PLANES - SIDE)]
    near_shot = [shot_at(1, 0), shot_at(LAYERS - 1, 0), shot_at(0, 1)]
    for peer in near_pen + near_shot:
        pl.semaphore_signal(barrier, inc=1, device_id=peer, device_id_type=MESH)

    for load in loads[1:]:
        load.start()

    greetings = [
        (0, near_pen),
        (1, near_shot),
        (2, [pen_at(SIDE), pen_at(PLANES - SIDE)]),
        (3, [shot_at(2, 0), shot_at(LAYERS - 2, 0)]),
        (4, [shot_at(0, 1)]),
    ]

    def greet(k):
        for peer in greetings[k][1]:
            pl.semaphore_signal(known.at[k], inc=1, device_id=peer, device_id_type=MESH)

    def greeted(k):
        pl.semaphore_wait(known.at[k], len(greetings[k][1]))

    first = aperture[0, 0]
    count = aperture[0, 1]
    window = jnp.minimum(first, NY // TILE - AMAX)
    low = first - window
    high = low + count
    start = window * TILE

    edge = jnp.zeros((8, NZ), jnp.float32)
    for ref in (ua, ub, ra, rb):
        ref[pl.ds(0, 8), :] = edge
        ref[pl.ds(ROWS + 8, 8), :] = edge

    lane = lax.broadcasted_iota(jnp.int32, (TILE, NZ), 1)
    row = lax.broadcasted_iota(jnp.int32, (TILE, NZ), 0)

    def pick(options, like):
        where_from = like * 0 + window
        out = options[SHIFTS - 1]
        for i in range(SHIFTS - 2, -1, -1):
            out = jnp.where(where_from == i, options[i], out)
        return out

    def take_window(b, places):
        row_here = row + b * TILE
        inside = (row_here >= low * TILE) & (row_here < high * TILE)
        for ref, lead, out, pad in places:
            options = [ref[(*lead, block_rows(b, i * TILE))] for i in range(SHIFTS)]
            out[block_rows(b, pad), :] = jnp.where(inside, pick(options, row), 0.0)

    def load_block(places):
        def body(b, carry):
            take_window(b, places)
            return carry

        lax.fori_loop(0, AMAX, body, 0)

    loads[0].wait()
    load_block([(source, (0,), ua, 8)])

    pl.semaphore_wait(barrier, len(near_pen) + len(near_shot))

    up, down = near_pen[0], near_pen[1]

    def exchange(body, low, high, send, recv):
        upward = pltpu.make_async_remote_copy(
            body, low, send.at[0], recv.at[0], device_id=up, device_id_type=MESH
        )
        downward = pltpu.make_async_remote_copy(
            body, high, send.at[1], recv.at[1], device_id=down, device_id_type=MESH
        )

        class Pair:
            def start(self):
                pl.when(pen < PLANES - 1)(upward.start)
                pl.when(pen > 0)(downward.start)

            def sent(self):
                pl.when(pen < PLANES - 1)(upward.wait_send)
                pl.when(pen > 0)(downward.wait_send)

            def arrived(self):
                pl.when(pen > 0)(upward.wait_recv)
                pl.when(pen < PLANES - 1)(downward.wait_recv)

        return Pair()

    def halo(state, slot):
        return exchange(
            state.at[pl.ds(8, ROWS), :],
            from_low.at[slot],
            from_high.at[slot],
            halo_send.at[slot],
            halo_recv.at[slot],
        )

    def halo_turned(k):
        at = pl.ds(k * DEEP, DEEP)
        return exchange(
            turned_u.at[at, :],
            low_turned.at[at, :],
            high_turned.at[at, :],
            last_send.at[k],
            last_recv.at[k],
        )

    not_first = lane > 0
    not_last = lane < NZ - 1

    def laplace(state, slot, b):
        wide = state[pl.ds(pl.multiple_of(b * TILE, TILE), TILE + 16), :]
        here = wide[8 : TILE + 8]
        at = block_rows(b)
        beside = pltpu.roll(wide, 1, 0)[8 : TILE + 8]
        beside = beside + pltpu.roll(wide, TILE + 15, 0)[8 : TILE + 8]
        beside = beside + jnp.where(not_first, pltpu.roll(here, 1, 1), 0.0)
        beside = beside + jnp.where(not_last, pltpu.roll(here, NZ - 1, 1), 0.0)
        if slot is not None:
            beside = beside + (from_low[slot, at, :] + from_high[slot, at, :])
        return here, beside - 6.0 * here

    def with_strips(b, moment, new):
        row_here = row + b * TILE
        for i in range(2):
            new = jnp.where(
                row_here == low * TILE + i, strips[moment, 0, pl.ds(i, 1), :], new
            )
            new = jnp.where(
                row_here == high * TILE - 2 + i, strips[moment, 1, pl.ds(i, 1), :], new
            )
        return new

    def columns(b, pad=0):
        return pl.ds(pl.multiple_of(b * TILE + pad, TILE), TILE)

    def source_step(now, old, slot, moment, adjoint_now):
        amplitude = wavelet[0, moment]

        def body(b, carry):
            here, lap = laplace(now, slot, b)
            at = block_rows(b)
            at8 = block_rows(b, 8)
            before = old[at8, :]
            new = 2.0 * here - before + cw[at, :] * (lap + amplitude * hit[at, :])
            new = with_strips(b, moment, new)
            at256 = block_rows(b, 2 * TILE)
            step = (before - 2.0 * here + new) * adjoint_now[at8, :]
            old[at8, :] = new
            if moment == 0:
                grad[at, :] = step
                light[at256, :] = here * here
            else:
                grad[at, :] = grad[at, :] + step
                light[at256, :] = light[at256, :] + here * here + new * new
                turned_u[:, columns(b)] = jnp.transpose(new)
            return carry

        lax.fori_loop(0, AMAX, body, 0)

    def last_step(now, old, moment, adjoint_now):
        amplitude = wavelet[0, moment]

        def body(b, carry):
            here, lap = laplace(now, None, b)
            at = block_rows(b)
            at8 = block_rows(b, 8)
            before = old[at8, :]
            new = 2.0 * here - before + cw[at, :] * (lap + amplitude * hit[at, :])
            new = with_strips(b, moment, new)
            free = cw[at, :]
            row_here = row + b * TILE
            for i in range(2):
                free = jnp.where(row_here == low * TILE + i, 0.0, free)
                free = jnp.where(row_here == high * TILE - 2 + i, 0.0, free)
            ahead = adjoint_now[at8, :]
            known_part = grad[at, :] + (before - 2.0 * here + new) * ahead
            whole[:, columns(b, 2 * TILE)] = jnp.transpose(known_part)
            slope[:, columns(b)] = jnp.transpose(free * ahead)
            return carry

        lax.fori_loop(0, AMAX, body, 0)

    def adjoint_step(now, old, slot, moment):
        def body(b, carry):
            here, lap = laplace(now, slot, b)
            at = block_rows(b)
            at8 = block_rows(b, 8)
            old[at8, :] = 2.0 * here - old[at8, :] + cw[at, :] * (lap + inj[moment, at, :])
            return carry

        lax.fori_loop(0, AMAX, body, 0)

    u0, r0, u1, r1 = halo(ua, 0), halo(ra, 1), halo(ub, 2), halo(rb, 3)
    u2 = [halo_turned(k) for k in range(QUARTERS)]
    u0.start()
    greet(0)
    greet(1)
    loads[1].wait()
    load_block([(source, (1,), ub, 8)])

    @pl.when(pen == 0)
    def _():
        from_low[...] = jnp.zeros_like(from_low)
        low_turned[...] = jnp.zeros_like(low_turned)

    @pl.when(pen == PLANES - 1)
    def _():
        from_high[...] = jnp.zeros_like(from_high)
        high_turned[...] = jnp.zeros_like(high_turned)

    loads[2].wait()
    load_block([(adjoint, (0,), ra, 8), (adjoint, (1,), rb, 8)])
    u0.sent()
    r0.start()
    for load in loads[3:]:
        load.wait()
    greeted(0)
    greeted(1)
    greet(2)
    greet(3)
    load_block([(courant, (), cw, 0)])

    cell_row = jnp.where(cells[pl.ds(0, 1), :] == pen, cells[pl.ds(1, 1), :] - start, -1)
    slab = lax.broadcasted_iota(jnp.int32, (8, NREC), 0)
    values = jnp.where(lax.rem(slab, 2) == 0, residuals[0], residuals[1])
    coarse = values.astype(jnp.bfloat16).astype(jnp.float32)
    middle = (values - coarse).astype(jnp.bfloat16).astype(jnp.float32)
    fine = values - coarse - middle
    values = jnp.where(slab < DEPTH + 2, coarse, jnp.where(slab < DEPTH + 4, middle, fine))
    values = jnp.where(slab < DEPTH, 0.0, values)
    values = jnp.concatenate([values, jnp.zeros((NZ - 8, NREC), jnp.float32)], axis=0)
    values = jnp.transpose(values).astype(jnp.bfloat16)
    rows_wide = lax.broadcasted_iota(jnp.int32, (TILE, NREC), 0)

    def inject_block(b, carry):
        chosen = jnp.where(rows_wide == cell_row - b * TILE, 1.0, 0.0).astype(jnp.bfloat16)
        out = jnp.dot(chosen, values, preferred_element_type=jnp.float32)
        out = out + pltpu.roll(out, NZ - 2, 1) + pltpu.roll(out, NZ - 4, 1)
        at = block_rows(b)
        inj[0, at, :] = jnp.where(lane == DEPTH, out, 0.0)
        inj[1, at, :] = jnp.where(lane == DEPTH, pltpu.roll(out, NZ - 1, 1), 0.0)
        key = row + (b * TILE + pen * NY)
        cell = source_cell[0, 0] * NY + source_cell[0, 1] - start
        here = (key == cell) & (lane == source_cell[0, 2])
        hit[at, :] = jnp.where(here, 1.0, 0.0)
        return carry

    lax.fori_loop(0, AMAX, inject_block, 0)
    light[pl.ds(0, 2 * TILE), :] = jnp.zeros((2 * TILE, NZ), jnp.float32)
    light[pl.ds(ROWS + 2 * TILE, 2 * TILE), :] = jnp.zeros((2 * TILE, NZ), jnp.float32)
    whole[:, pl.ds(0, 2 * TILE)] = jnp.zeros((NZ, 2 * TILE), jnp.float32)
    whole[:, pl.ds(ROWS + 2 * TILE, 2 * TILE)] = jnp.zeros((NZ, 2 * TILE), jnp.float32)
    greeted(2)
    greeted(3)
    greet(4)

    def spread_light():
        def body(g, carry):
            options = []
            for shift in range(SHIFTS):
                options.append(light[block_rows(g, (SHIFTS - 1 - shift) * TILE), :])
            flat = jnp.transpose(pick(options, row))
            for d in range(SHOTS):
                k, j = d // 4, d % 4
                split_l[j % 2, k, j // 2, :, columns(g)] = flat[8 * d : 8 * d + 8]
            return carry

        lax.fori_loop(0, NY // TILE, body, 0)

    def spread_quarter(k):
        at = pl.ds(k * DEEP, DEEP)
        inner = pl.ds(2 * TILE, ROWS)
        pushed = low_turned[at, :] + high_turned[at, :]
        whole[at, inner] = whole[at, inner] + slope[at, :] * pushed
        for j in range(4):
            rows8 = pl.ds(k * DEEP + 8 * j, 8)
            options = []
            for shift in range(SHIFTS):
                options.append(whole[rows8, pl.ds((SHIFTS - 1 - shift) * TILE, NY)])
            like = lax.broadcasted_iota(jnp.int32, (8, NY), 0)
            split_g[j % 2, k, j // 2] = pick(options, like)

    class Sum:
        def __init__(self, split, pair, mine, ring, which):
            self.split, self.pair, self.mine, self.ring = split, pair, mine, ring
            self.pairs, self.targets = [], []
            for k in range(QUARTERS):
                self.pairs.append(
                    pltpu.make_async_remote_copy(
                        split.at[1 - core, k], pair.at[k], pair_send.at[which, k],
                        pair_recv.at[which, k],
                        device_id=shot_at(0, 1), device_id_type=MESH,
                    )
                )
                for h in range(2):
                    target = k + 4 * h
                    slot = lax.rem(target - z + 2 * LAYERS - 1, LAYERS)
                    self.targets.append(
                        pltpu.make_async_remote_copy(
                            mine.at[k, h], ring.at[slot], ring_send.at[which, target],
                            ring_recv.at[which, slot],
                            device_id=(2 * target + core, pen), device_id_type=MESH,
                        )
                    )
            self.arrivals = [
                pltpu.make_async_remote_copy(
                    mine.at[0, 0], ring.at[slot], ring_send.at[which, 0],
                    ring_recv.at[which, slot],
                    device_id=shot_at(1, 0), device_id_type=MESH,
                )
                for slot in range(LAYERS - 1)
            ]

        def start_ring(self, k):
            self.pairs[k].wait()
            self.mine[k] = self.split[core, k] + self.pair[k]
            for h in range(2):
                pl.when(z != k + 4 * h)(self.targets[2 * k + h].start)

        def finish(self):
            total_here = self.mine[lax.rem(z, 4), z // 4]
            for slot in range(LAYERS - 1):
                self.arrivals[slot].wait_recv()
                total_here = total_here + self.ring[slot]
            for k in range(QUARTERS):
                for h in range(2):
                    pl.when(z != k + 4 * h)(self.targets[2 * k + h].wait_send)
            return total_here

    sum_l = Sum(split_l, pair_l, mine_l, ring_l, 0)
    sum_g = Sum(split_g, pair_g, mine_g, ring_g, 1)

    u0.arrived()
    source_step(ua, ub, 0, 0, ra)
    r0.sent()
    u1.start()
    greeted(4)
    r0.arrived()
    adjoint_step(ra, rb, 1, 0)
    u1.sent()
    r1.start()

    def cut_block(g, carry):
        at = block_rows(g)
        waves_cut[at, :] = jnp.concatenate(cut_in_two(table[at, :]), axis=1)
        return carry

    lax.fori_loop(0, NY // TILE, cut_block, 0)
    z_cut[...] = jnp.concatenate(cut_in_two(table[pl.ds(NY, NZ), :]), axis=1)
    rows_here = pl.ds(pl.multiple_of(shot * CHUNK, CHUNK), CHUNK)
    mine_cut[...] = jnp.concatenate(cut_in_two(table[rows_here, :]), axis=0)
    u1.arrived()
    source_step(ub, ua, 2, 1, rb)
    spread_light()
    for k in range(QUARTERS):
        sum_l.pairs[k].start()
    for k in range(QUARTERS):
        sum_l.start_ring(k)
    r1.sent()
    u2[0].start()
    u2[1].start()
    r1.arrived()
    adjoint_step(rb, ra, 3, 1)
    u2[0].sent()
    u2[2].start()
    last_step(ua, ub, 2, ra)
    u2[1].sent()
    u2[3].start()
    for k in range(QUARTERS):
        u2[k].arrived()
        spread_quarter(k)
        sum_g.pairs[k].start()
        if k > 0:
            sum_g.start_ring(k - 1)
    sum_g.start_ring(QUARTERS - 1)
    for k in range(2, QUARTERS):
        u2[k].sent()
    lighting = sum_l.finish()
    gradient = sum_g.finish()
    precond = gradient / (lighting + DAMPING)
    for h in range(LAYERS):
        tiles[h] = precond[:, h * TILE : (h + 1) * TILE]

    def over_layers(origin, place, send, recv):
        copies = []
        for i, d in enumerate((4, 3, 5, 2, 6, 1, 7)):
            copies.append(
                pltpu.make_async_remote_copy(
                    origin(lax.rem(z + d, LAYERS)), place.at[core, z], send.at[i], recv.at[i],
                    device_id=shot_at(d, 0), device_id_type=MESH,
                )
            )
        return copies

    def to_partner(place, send, recv):
        return pltpu.make_async_remote_copy(
            place.at[core], place.at[core], send.at[LAYERS - 1], recv.at[LAYERS - 1],
            device_id=shot_at(0, 1), device_id_type=MESH,
        )

    tile_copies = over_layers(lambda layer: tiles.at[layer], tiles_in, tiles_send, tiles_recv)
    tile_pair = to_partner(tiles_in, tiles_send, tiles_recv)
    tally = jnp.dot(
        jnp.concatenate(cut_in_two(precond), axis=0),
        waves_cut[...],
        preferred_element_type=jnp.float32,
    )
    tally = four_sums(tally, 8)
    coef[...] = tally
    copies = []
    for i, rel in enumerate(PEN_REL):
        copies.append(
            pltpu.make_async_remote_copy(
                coef, coef_in.at[i], coef_send.at[i], coef_recv.at[i],
                device_id=pen_peer(rel), device_id_type=MESH,
            )
        )
    for copy in copies:
        copy.start()
    for copy in tile_copies:
        copy.start()
    tiles_in[core, z] = tiles[z]
    mixed = tally * gauss[pen, pen]
    for i, (dy, dx) in enumerate(PEN_REL):
        copies[i].wait_recv()
        origin = lax.rem(py + SIDE - dy, SIDE) * SIDE + lax.rem(px + SIDE - dx, SIDE)
        mixed = mixed + coef_in[i] * gauss[pen, origin]
    coef_copies = copies
    total[core, z] = mixed * table[pl.ds(NY + NZ, 8), :]
    copies = []
    for i, (dz, dc) in enumerate(SHOT_REL):
        copies.append(
            pltpu.make_async_remote_copy(
                total.at[core, z], total.at[core, z], total_send.at[i], total_recv.at[i],
                device_id=shot_at(dz, dc), device_id_type=MESH,
            )
        )
    for copy in copies:
        copy.start()
    for copy in tile_copies:
        copy.wait_recv()
    tile_pair.start()
    for copy in coef_copies + tile_copies:
        copy.wait_send()
    tile_pair.wait()
    stack = []
    for d in range(SHOTS):
        stack.append(tiles_in[d % 2, d // 4 + 4 * ((d % 4) // 2)])
    turned[...] = jnp.transpose(jnp.concatenate(stack, axis=0))
    both_out[0] = turned[pl.ds(pl.multiple_of(core * CHUNK, CHUNK), CHUNK), :]
    for copy in copies:
        copy.wait_recv()
    wide = lax.dot_general(
        mine_cut[...],
        jnp.concatenate(cut_in_two(total[...].reshape(NZ, MODES)), axis=0),
        (((1,), (1,)), ((), ())),
        preferred_element_type=jnp.float32,
    )
    wide = four_sums(wide, CHUNK)
    smooth = jnp.dot(
        jnp.concatenate(cut_in_two(wide), axis=0),
        z_cut[...],
        preferred_element_type=jnp.float32,
    )
    both_out[1] = four_sums(smooth, CHUNK)
    for copy in copies:
        copy.wait_send()


def on_device(
    courant,
    source_states,
    adjoint_states,
    strips,
    aperture,
    source_cell,
    wavelet,
    receiver_cells,
    residuals,
):
    table = operator_table()
    vmem = pl.BlockSpec(memory_space=pltpu.VMEM)
    hbm = pl.BlockSpec(memory_space=pltpu.HBM)
    smem = pl.BlockSpec(memory_space=pltpu.SMEM)
    f32 = jnp.float32
    dma = pltpu.SemaphoreType.DMA
    others = SHOTS - 1
    state = pltpu.VMEM((ROWS + 16, NZ), f32)
    field = pltpu.VMEM((ROWS, NZ), f32)
    both = pl.pallas_call(
        kernel,
        out_shape=jax.ShapeDtypeStruct((2, CHUNK, NZ), f32),
        in_specs=[smem] * 4 + [hbm] * 7,
        out_specs=vmem,
        scratch_shapes=[
            pltpu.VMEM((NY, NZ), f32),
            pltpu.VMEM((2, NY, NZ), f32),
            pltpu.VMEM((2, NY, NZ), f32),
            pltpu.VMEM((STEPS, 2, 2, NZ), f32),
            pltpu.VMEM((2, NREC), jnp.int32),
            pltpu.VMEM((STEPS, 1, NREC), f32),
            pltpu.VMEM(table.shape, f32),
            state,
            state,
            state,
            state,
            field,
            field,
            pltpu.VMEM((2, ROWS, NZ), f32),
            pltpu.VMEM((4, ROWS, NZ), f32),
            pltpu.VMEM((4, ROWS, NZ), f32),
            field,
            pltpu.VMEM((ROWS + 4 * TILE, NZ), f32),
            pltpu.VMEM((NZ, ROWS), f32),
            pltpu.VMEM((NZ, ROWS), f32),
            pltpu.VMEM((NZ, ROWS), f32),
            pltpu.VMEM((NZ, ROWS), f32),
            pltpu.VMEM((NZ, ROWS + 4 * TILE), f32),
            pltpu.VMEM((2, QUARTERS, 2, 8, NY), f32),
            pltpu.VMEM((2, QUARTERS, 2, 8, NY), f32),
            pltpu.VMEM((QUARTERS, 2, 8, NY), f32),
            pltpu.VMEM((QUARTERS, 2, 8, NY), f32),
            pltpu.VMEM((QUARTERS, 2, 8, NY), f32),
            pltpu.VMEM((QUARTERS, 2, 8, NY), f32),
            pltpu.VMEM((LAYERS, 8, NY), f32),
            pltpu.VMEM((LAYERS, 8, NY), f32),
            pltpu.VMEM((LAYERS, 8, TILE), f32),
            pltpu.VMEM((2, LAYERS, 8, TILE), f32),
            pltpu.VMEM((TILE, NZ), f32),
            pltpu.VMEM((8, NZ), f32),
            pltpu.VMEM((others, 8, NZ), f32),
            pltpu.VMEM((2, LAYERS, 8, NZ), f32),
            pltpu.VMEM((NY, 2 * MODES), jnp.bfloat16),
            pltpu.VMEM((2 * CHUNK, MODES), jnp.bfloat16),
            pltpu.VMEM((NZ, 2 * NZ), jnp.bfloat16),
            pltpu.SemaphoreType.REGULAR((5,)),
            dma((8,)),
            dma((QUARTERS, 2)),
            dma((QUARTERS, 2)),
            dma((4, 2)),
            dma((4, 2)),
            dma((2, QUARTERS)),
            dma((2, QUARTERS)),
            dma((2, LAYERS)),
            dma((2, LAYERS)),
            dma((LAYERS,)),
            dma((LAYERS,)),
            dma((others,)),
            dma((others,)),
            dma((others,)),
            dma((others,)),
        ],
        compiler_params=pltpu.CompilerParams(
            collective_id=0, has_side_effects=True, vmem_limit_bytes=63 << 20
        ),
        name="inversion",
    )(
        aperture,
        source_cell,
        wavelet,
        jnp.asarray(gauss_table(PLANES, float(PLANES) / 4.0)),
        courant[0],
        source_states[0, :, 0],
        adjoint_states[0, :, 0],
        strips[0, :, :, 0],
        receiver_cells[0].T,
        residuals.transpose(1, 0, 2),
        jnp.asarray(table),
    )
    return (both[0:1], both[1:2])


def solution(mesh):
    placed = (
        P("pen", None, None),
        P("shot", None, "pen", None, None),
        P("shot", None, "pen", None, None),
        P("shot", None, None, "pen", None, None),
        P("shot", None),
        P("shot", None),
        P("shot", None),
        P("shot", None, None),
        P("shot", None, None),
    )
    return jax.shard_map(
        on_device,
        mesh=mesh,
        in_specs=placed,
        out_specs=(P("pen", "shot", None), P("pen", "shot", None)),
        check_vma=False,
    )
```

```python
import math

import jax
import jax.numpy as jnp
import numpy as np
from jax import lax
from jax.experimental import pallas as pl
from jax.experimental.pallas import tpu as pltpu
from jax.sharding import PartitionSpec as P

TILE = 128
NY = 1024
NZ = 128
AMAX = 6
STEPS = 3
NREC = 512
SHOTS = 16
PLANES = 16
ROWS = AMAX * TILE
CHUNK = NY // SHOTS
MODES = 128
DEPTH = 2
SHIFTS = NY // TILE - AMAX + 1
QUARTERS = 4
DEEP = NZ // QUARTERS
DAMPING = 1.0
SIGMA_Z = 4.0
MESH = pl.DeviceIdType.MESH
HIGHEST = lax.Precision.HIGHEST
LAYERS = 8
SIDE = 4


def hops(*steps):
    return -sum(min(step, size - step) for step, size in steps)


PEN_REL = sorted(
    [(dy, dx) for dy in range(SIDE) for dx in range(SIDE) if (dy, dx) != (0, 0)],
    key=lambda rel: hops((rel[0], SIDE), (rel[1], SIDE)),
)

SHOT_REL = sorted(
    [(dz, dc) for dz in range(LAYERS) for dc in range(2) if (dz, dc) != (0, 0)],
    key=lambda rel: hops((rel[0], LAYERS), (rel[1], 2)),
)


def wave_table(length, spread):
    half = MODES // 2
    order = np.concatenate([np.arange(half), np.arange(1, half + 1)])
    angle = 2.0 * np.pi * ((order[:, None] * np.arange(length)[None, :]) % length) / length
    waves = np.where(np.arange(2 * half)[:, None] < half, np.cos(angle), np.sin(angle))
    weights = np.exp(-0.5 * (spread * 2.0 * np.pi * order / length) ** 2) / length
    weights = np.where(order == 0, weights, 2.0 * weights)
    return waves.T, weights


def circulant_table(length, spread):
    frequency = np.fft.fftfreq(length)
    weights = np.exp(-0.5 * (spread * 2.0 * np.pi * frequency) ** 2)
    vector = np.real(np.fft.ifft(weights))
    position = np.arange(length)
    return vector[(position[:, None] - position[None, :]) % length].astype(np.float32)


def gauss_table(total, spread):
    position = np.arange(total)
    distance = (position[:, None] - position[None, :]).astype(np.float64)
    table = np.exp(-0.5 * (distance / spread) ** 2) / (spread * math.sqrt(2.0 * math.pi))
    return table.astype(np.float32)


def depth_slot(layer, core):
    return 8 * (layer % 2) + 4 * core + layer // 2


def operator_table():
    waves, weights = wave_table(NY, float(NY) / float(SHOTS))
    owners = [(core, layer) for core in range(2) for layer in range(LAYERS)]
    depths = [8 * depth_slot(layer, core) + i for core, layer in owners for i in range(8)]
    z_part = circulant_table(NZ, SIGMA_Z)[np.array(depths)]
    return np.concatenate([waves, z_part, np.tile(weights, (8, 1))]).astype(np.float32)


def cut_in_two(value):
    coarse = value.astype(jnp.bfloat16)
    return coarse, (value - coarse.astype(jnp.float32)).astype(jnp.bfloat16)


def four_sums(out, rows):
    first = out[:rows, :NZ] + (out[:rows, NZ:] + out[rows:, :NZ])
    return first + out[rows:, NZ:]


def block_rows(b, pad=0):
    return pl.ds(pl.multiple_of(b * TILE + pad, 8), TILE)


def kernel(
    aperture,
    source_cell,
    wavelet,
    gauss,
    courant_hbm,
    source_hbm,
    adjoint_hbm,
    strips_hbm,
    cells_hbm,
    residuals_hbm,
    table_hbm,
    both_out,
    courant,
    source,
    adjoint,
    strips,
    cells,
    residuals,
    table,
    ua,
    ub,
    ra,
    rb,
    cw,
    hit,
    inj,
    from_low,
    from_high,
    grad,
    light,
    turned_u,
    low_turned,
    high_turned,
    slope,
    whole,
    split_g,
    split_l,
    pair_g,
    pair_l,
    mine_g,
    mine_l,
    ring_g,
    ring_l,
    tiles,
    tiles_in,
    turned,
    coef,
    coef_in,
    total,
    waves_cut,
    mine_cut,
    z_cut,
    known,
    load_sem,
    last_send,
    last_recv,
    halo_send,
    halo_recv,
    pair_send,
    pair_recv,
    ring_send,
    ring_recv,
    tiles_send,
    tiles_recv,
    coef_send,
    coef_recv,
    total_send,
    total_recv,
):
    shot = lax.axis_index("shot")
    pen = lax.axis_index("pen")
    z, core = shot // 2, lax.rem(shot, 2)
    py, px = pen // SIDE, lax.rem(pen, SIDE)

    def pen_peer(rel):
        dy, dx = rel
        return (shot, lax.rem(py + dy, SIDE) * SIDE + lax.rem(px + dx, SIDE))

    loads = []
    for i, (origin, place) in enumerate(
        (
            (source_hbm.at[0], source.at[0]),
            (source_hbm.at[1], source.at[1]),
            (adjoint_hbm, adjoint),
            (courant_hbm, courant),
            (cells_hbm, cells),
            (residuals_hbm, residuals),
            (strips_hbm, strips),
            (table_hbm, table),
        )
    ):
        loads.append(pltpu.make_async_copy(origin, place, load_sem.at[i]))
    loads[0].start()

    barrier = pltpu.get_barrier_semaphore()
    def pen_at(offset):
        return (shot, lax.rem(pen + offset, PLANES))

    def shot_at(dz, dc):
        return (lax.rem(z + dz, LAYERS) * 2 + lax.rem(core + dc, 2), pen)

    near_pen = [pen_at(o) for o in (1, PLANES - 1, SIDE, PLANES - SIDE)]
    near_shot = [shot_at(1, 0), shot_at(LAYERS - 1, 0), shot_at(0, 1)]
    for peer in near_pen + near_shot:
        pl.semaphore_signal(barrier, inc=1, device_id=peer, device_id_type=MESH)

    for load in loads[1:]:
        load.start()

    greetings = [
        (0, near_pen),
        (1, near_shot),
        (2, [pen_at(SIDE), pen_at(PLANES - SIDE)]),
        (3, [shot_at(2, 0), shot_at(LAYERS - 2, 0)]),
        (4, [shot_at(0, 1)]),
    ]

    def greet(k):
        for peer in greetings[k][1]:
            pl.semaphore_signal(known.at[k], inc=1, device_id=peer, device_id_type=MESH)

    def greeted(k):
        pl.semaphore_wait(known.at[k], len(greetings[k][1]))

    first = aperture[0, 0]
    count = aperture[0, 1]
    window = jnp.minimum(first, NY // TILE - AMAX)
    low = first - window
    high = low + count
    start = window * TILE

    edge = jnp.zeros((8, NZ), jnp.float32)
    for ref in (ua, ub, ra, rb):
        ref[pl.ds(0, 8), :] = edge
        ref[pl.ds(ROWS + 8, 8), :] = edge

    lane = lax.broadcasted_iota(jnp.int32, (TILE, NZ), 1)
    row = lax.broadcasted_iota(jnp.int32, (TILE, NZ), 0)

    def pick(options, like):
        where_from = like * 0 + window
        out = options[SHIFTS - 1]
        for i in range(SHIFTS - 2, -1, -1):
            out = jnp.where(where_from == i, options[i], out)
        return out

    def take_window(b, places):
        row_here = row + b * TILE
        inside = (row_here >= low * TILE) & (row_here < high * TILE)
        for ref, lead, out, pad in places:
            options = [ref[(*lead, block_rows(b, i * TILE))] for i in range(SHIFTS)]
            out[block_rows(b, pad), :] = jnp.where(inside, pick(options, row), 0.0)

    def load_block(places):
        def body(b, carry):
            take_window(b, places)
            return carry

        lax.fori_loop(0, AMAX, body, 0)

    loads[0].wait()
    load_block([(source, (0,), ua, 8)])

    pl.semaphore_wait(barrier, len(near_pen) + len(near_shot))

    up, down = near_pen[0], near_pen[1]

    def exchange(body, low, high, send, recv):
        upward = pltpu.make_async_remote_copy(
            body, low, send.at[0], recv.at[0], device_id=up, device_id_type=MESH
        )
        downward = pltpu.make_async_remote_copy(
            body, high, send.at[1], recv.at[1], device_id=down, device_id_type=MESH
        )

        class Pair:
            def start(self):
                pl.when(pen < PLANES - 1)(upward.start)
                pl.when(pen > 0)(downward.start)

            def sent(self):
                pl.when(pen < PLANES - 1)(upward.wait_send)
                pl.when(pen > 0)(downward.wait_send)

            def arrived(self):
                pl.when(pen > 0)(upward.wait_recv)
                pl.when(pen < PLANES - 1)(downward.wait_recv)

        return Pair()

    def halo(state, slot):
        return exchange(
            state.at[pl.ds(8, ROWS), :],
            from_low.at[slot],
            from_high.at[slot],
            halo_send.at[slot],
            halo_recv.at[slot],
        )

    def halo_turned(k):
        at = pl.ds(k * DEEP, DEEP)
        return exchange(
            turned_u.at[at, :],
            low_turned.at[at, :],
            high_turned.at[at, :],
            last_send.at[k],
            last_recv.at[k],
        )

    not_first = lane > 0
    not_last = lane < NZ - 1

    def laplace(state, slot, b):
        wide = state[pl.ds(pl.multiple_of(b * TILE, TILE), TILE + 16), :]
        here = wide[8 : TILE + 8]
        at = block_rows(b)
        beside = pltpu.roll(wide, 1, 0)[8 : TILE + 8]
        beside = beside + pltpu.roll(wide, TILE + 15, 0)[8 : TILE + 8]
        beside = beside + jnp.where(not_first, pltpu.roll(here, 1, 1), 0.0)
        beside = beside + jnp.where(not_last, pltpu.roll(here, NZ - 1, 1), 0.0)
        if slot is not None:
            beside = beside + (from_low[slot, at, :] + from_high[slot, at, :])
        return here, beside - 6.0 * here

    def with_strips(b, moment, new):
        row_here = row + b * TILE
        for i in range(2):
            new = jnp.where(
                row_here == low * TILE + i, strips[moment, 0, pl.ds(i, 1), :], new
            )
            new = jnp.where(
                row_here == high * TILE - 2 + i, strips[moment, 1, pl.ds(i, 1), :], new
            )
        return new

    def columns(b, pad=0):
        return pl.ds(pl.multiple_of(b * TILE + pad, TILE), TILE)

    def source_step(now, old, slot, moment, adjoint_now):
        amplitude = wavelet[0, moment]

        def body(b, carry):
            here, lap = laplace(now, slot, b)
            at = block_rows(b)
            at8 = block_rows(b, 8)
            before = old[at8, :]
            new = 2.0 * here - before + cw[at, :] * (lap + amplitude * hit[at, :])
            new = with_strips(b, moment, new)
            at256 = block_rows(b, 2 * TILE)
            step = (before - 2.0 * here + new) * adjoint_now[at8, :]
            old[at8, :] = new
            if moment == 0:
                grad[at, :] = step
                light[at256, :] = here * here
            else:
                grad[at, :] = grad[at, :] + step
                light[at256, :] = light[at256, :] + here * here + new * new
                turned_u[:, columns(b)] = jnp.transpose(new)
            return carry

        lax.fori_loop(0, AMAX, body, 0)

    def last_step(now, old, moment, adjoint_now):
        amplitude = wavelet[0, moment]

        def body(b, carry):
            here, lap = laplace(now, None, b)
            at = block_rows(b)
            at8 = block_rows(b, 8)
            before = old[at8, :]
            new = 2.0 * here - before + cw[at, :] * (lap + amplitude * hit[at, :])
            new = with_strips(b, moment, new)
            free = cw[at, :]
            row_here = row + b * TILE
            for i in range(2):
                free = jnp.where(row_here == low * TILE + i, 0.0, free)
                free = jnp.where(row_here == high * TILE - 2 + i, 0.0, free)
            ahead = adjoint_now[at8, :]
            known_part = grad[at, :] + (before - 2.0 * here + new) * ahead
            whole[:, columns(b, 2 * TILE)] = jnp.transpose(known_part)
            slope[:, columns(b)] = jnp.transpose(free * ahead)
            return carry

        lax.fori_loop(0, AMAX, body, 0)

    def adjoint_step(now, old, slot, moment):
        def body(b, carry):
            here, lap = laplace(now, slot, b)
            at = block_rows(b)
            at8 = block_rows(b, 8)
            old[at8, :] = 2.0 * here - old[at8, :] + cw[at, :] * (lap + inj[moment, at, :])
            return carry

        lax.fori_loop(0, AMAX, body, 0)

    u0, r0, u1, r1 = halo(ua, 0), halo(ra, 1), halo(ub, 2), halo(rb, 3)
    u2 = [halo_turned(k) for k in range(QUARTERS)]
    u0.start()
    greet(0)
    greet(1)
    loads[1].wait()
    load_block([(source, (1,), ub, 8)])

    @pl.when(pen == 0)
    def _():
        from_low[...] = jnp.zeros_like(from_low)
        low_turned[...] = jnp.zeros_like(low_turned)

    @pl.when(pen == PLANES - 1)
    def _():
        from_high[...] = jnp.zeros_like(from_high)
        high_turned[...] = jnp.zeros_like(high_turned)

    loads[2].wait()
    load_block([(adjoint, (0,), ra, 8), (adjoint, (1,), rb, 8)])
    u0.sent()
    r0.start()
    for load in loads[3:]:
        load.wait()
    greeted(0)
    greeted(1)
    greet(2)
    greet(3)
    load_block([(courant, (), cw, 0)])

    cell_row = jnp.where(cells[pl.ds(0, 1), :] == pen, cells[pl.ds(1, 1), :] - start, -1)
    slab = lax.broadcasted_iota(jnp.int32, (8, NREC), 0)
    values = jnp.where(lax.rem(slab, 2) == 0, residuals[0], residuals[1])
    coarse = values.astype(jnp.bfloat16).astype(jnp.float32)
    middle = (values - coarse).astype(jnp.bfloat16).astype(jnp.float32)
    fine = values - coarse - middle
    values = jnp.where(slab < DEPTH + 2, coarse, jnp.where(slab < DEPTH + 4, middle, fine))
    values = jnp.where(slab < DEPTH, 0.0, values)
    values = jnp.concatenate([values, jnp.zeros((NZ - 8, NREC), jnp.float32)], axis=0)
    values = jnp.transpose(values).astype(jnp.bfloat16)
    rows_wide = lax.broadcasted_iota(jnp.int32, (TILE, NREC), 0)

    def inject_block(b, carry):
        chosen = jnp.where(rows_wide == cell_row - b * TILE, 1.0, 0.0).astype(jnp.bfloat16)
        out = jnp.dot(chosen, values, preferred_element_type=jnp.float32)
        out = out + pltpu.roll(out, NZ - 2, 1) + pltpu.roll(out, NZ - 4, 1)
        at = block_rows(b)
        inj[0, at, :] = jnp.where(lane == DEPTH, out, 0.0)
        inj[1, at, :] = jnp.where(lane == DEPTH, pltpu.roll(out, NZ - 1, 1), 0.0)
        key = row + (b * TILE + pen * NY)
        cell = source_cell[0, 0] * NY + source_cell[0, 1] - start
        here = (key == cell) & (lane == source_cell[0, 2])
        hit[at, :] = jnp.where(here, 1.0, 0.0)
        return carry

    lax.fori_loop(0, AMAX, inject_block, 0)
    light[pl.ds(0, 2 * TILE), :] = jnp.zeros((2 * TILE, NZ), jnp.float32)
    light[pl.ds(ROWS + 2 * TILE, 2 * TILE), :] = jnp.zeros((2 * TILE, NZ), jnp.float32)
    whole[:, pl.ds(0, 2 * TILE)] = jnp.zeros((NZ, 2 * TILE), jnp.float32)
    whole[:, pl.ds(ROWS + 2 * TILE, 2 * TILE)] = jnp.zeros((NZ, 2 * TILE), jnp.float32)
    greeted(2)
    greeted(3)
    greet(4)

    def spread_light():
        def body(g, carry):
            options = []
            for shift in range(SHIFTS):
                options.append(light[block_rows(g, (SHIFTS - 1 - shift) * TILE), :])
            flat = jnp.transpose(pick(options, row))
            for d in range(SHOTS):
                k, j = d // 4, d % 4
                split_l[k, j, :, columns(g)] = flat[8 * d : 8 * d + 8]
            return carry

        lax.fori_loop(0, NY // TILE, body, 0)

    def spread_quarter(k):
        at = pl.ds(k * DEEP, DEEP)
        inner = pl.ds(2 * TILE, ROWS)
        pushed = low_turned[at, :] + high_turned[at, :]
        whole[at, inner] = whole[at, inner] + slope[at, :] * pushed
        for j in range(4):
            rows8 = pl.ds(k * DEEP + 8 * j, 8)
            options = []
            for shift in range(SHIFTS):
                options.append(whole[rows8, pl.ds((SHIFTS - 1 - shift) * TILE, NY)])
            like = lax.broadcasted_iota(jnp.int32, (8, NY), 0)
            split_g[k, j] = pick(options, like)

    class Sum:
        def __init__(self, split, pair, mine, ring, which):
            self.split, self.pair, self.mine, self.ring = split, pair, mine, ring
            self.pairs, self.targets = [], []
            for k in range(QUARTERS):
                self.pairs.append(
                    pltpu.make_async_remote_copy(
                        split.at[k], pair.at[k // 2], pair_send.at[which, k],
                        pair_recv.at[which, k],
                        device_id=shot_at(0, 1), device_id_type=MESH,
                    )
                )
                for j in range(4):
                    target = k // 2 + 2 * j
                    slot = lax.rem(target - z + 2 * LAYERS - 1, LAYERS)
                    copy = pltpu.make_async_remote_copy(
                        mine.at[k // 2, j], ring.at[slot], ring_send.at[which, target],
                        ring_recv.at[which, slot],
                        device_id=(2 * target + k % 2, pen), device_id_type=MESH,
                    )
                    self.targets.append(((core == k % 2) & (z != target), copy))
            self.arrivals = [
                pltpu.make_async_remote_copy(
                    mine.at[0, 0], ring.at[slot], ring_send.at[which, 0],
                    ring_recv.at[which, slot],
                    device_id=shot_at(1, 0), device_id_type=MESH,
                )
                for slot in range(LAYERS - 1)
            ]

        def start_pair(self, k):
            pl.when(core != k % 2)(self.pairs[k].start)

        def start_ring(self, k):
            @pl.when(core == k % 2)
            def _():
                self.pairs[k].wait_recv()
                self.mine[k // 2] = self.split[k] + self.pair[k // 2]

            for there, copy in self.targets[4 * k : 4 * k + 4]:
                pl.when(there)(copy.start)

        def finish(self):
            total_here = self.mine[lax.rem(z, 2), z // 2]
            for slot in range(LAYERS - 1):
                self.arrivals[slot].wait_recv()
                total_here = total_here + self.ring[slot]
            for there, copy in self.targets:
                pl.when(there)(copy.wait_send)
            for k in range(QUARTERS):
                pl.when(core != k % 2)(self.pairs[k].wait_send)
            return total_here

    sum_l = Sum(split_l, pair_l, mine_l, ring_l, 0)
    sum_g = Sum(split_g, pair_g, mine_g, ring_g, 1)

    u0.arrived()
    source_step(ua, ub, 0, 0, ra)
    r0.sent()
    u1.start()
    greeted(4)
    r0.arrived()
    adjoint_step(ra, rb, 1, 0)
    u1.sent()
    r1.start()

    def cut_block(g, carry):
        at = block_rows(g)
        waves_cut[at, :] = jnp.concatenate(cut_in_two(table[at, :]), axis=1)
        return carry

    lax.fori_loop(0, NY // TILE, cut_block, 0)
    z_cut[...] = jnp.concatenate(cut_in_two(table[pl.ds(NY, NZ), :]), axis=1)
    rows_here = pl.ds(pl.multiple_of(shot * CHUNK, CHUNK), CHUNK)
    mine_cut[...] = jnp.concatenate(cut_in_two(table[rows_here, :]), axis=0)
    u1.arrived()
    source_step(ub, ua, 2, 1, rb)
    spread_light()
    for k in range(QUARTERS):
        sum_l.start_pair(k)
    for k in range(QUARTERS):
        sum_l.start_ring(k)
    r1.sent()
    u2[0].start()
    u2[1].start()
    r1.arrived()
    adjoint_step(rb, ra, 3, 1)
    u2[0].sent()
    u2[2].start()
    last_step(ua, ub, 2, ra)
    u2[1].sent()
    u2[3].start()
    for k in range(QUARTERS):
        u2[k].arrived()
        spread_quarter(k)
        sum_g.start_pair(k)
        if k > 0:
            sum_g.start_ring(k - 1)
    sum_g.start_ring(QUARTERS - 1)
    for k in range(2, QUARTERS):
        u2[k].sent()
    lighting = sum_l.finish()
    gradient = sum_g.finish()
    precond = gradient / (lighting + DAMPING)
    for h in range(LAYERS):
        tiles[h] = precond[:, h * TILE : (h + 1) * TILE]

    def over_layers(origin, place, send, recv):
        copies = []
        for i, d in enumerate((4, 3, 5, 2, 6, 1, 7)):
            copies.append(
                pltpu.make_async_remote_copy(
                    origin(lax.rem(z + d, LAYERS)), place.at[core, z], send.at[i], recv.at[i],
                    device_id=shot_at(d, 0), device_id_type=MESH,
                )
            )
        return copies

    def to_partner(place, send, recv):
        return pltpu.make_async_remote_copy(
            place.at[core], place.at[core], send.at[LAYERS - 1], recv.at[LAYERS - 1],
            device_id=shot_at(0, 1), device_id_type=MESH,
        )

    tile_copies = over_layers(lambda layer: tiles.at[layer], tiles_in, tiles_send, tiles_recv)
    tile_pair = to_partner(tiles_in, tiles_send, tiles_recv)
    tally = jnp.dot(
        jnp.concatenate(cut_in_two(precond), axis=0),
        waves_cut[...],
        preferred_element_type=jnp.float32,
    )
    tally = four_sums(tally, 8)
    coef[...] = tally
    copies = []
    for i, rel in enumerate(PEN_REL):
        copies.append(
            pltpu.make_async_remote_copy(
                coef, coef_in.at[i], coef_send.at[i], coef_recv.at[i],
                device_id=pen_peer(rel), device_id_type=MESH,
            )
        )
    for copy in copies:
        copy.start()
    for copy in tile_copies:
        copy.start()
    tiles_in[core, z] = tiles[z]
    mixed = tally * gauss[pen, pen]
    for i, (dy, dx) in enumerate(PEN_REL):
        copies[i].wait_recv()
        origin = lax.rem(py + SIDE - dy, SIDE) * SIDE + lax.rem(px + SIDE - dx, SIDE)
        mixed = mixed + coef_in[i] * gauss[pen, origin]
    coef_copies = copies
    total[core, z] = mixed * table[pl.ds(NY + NZ, 8), :]
    copies = []
    for i, (dz, dc) in enumerate(SHOT_REL):
        copies.append(
            pltpu.make_async_remote_copy(
                total.at[core, z], total.at[core, z], total_send.at[i], total_recv.at[i],
                device_id=shot_at(dz, dc), device_id_type=MESH,
            )
        )
    for copy in copies:
        copy.start()
    for copy in tile_copies:
        copy.wait_recv()
    tile_pair.start()
    for copy in coef_copies + tile_copies:
        copy.wait_send()
    tile_pair.wait()
    stack = []
    for d in range(SHOTS):
        stack.append(tiles_in[(d // 4) % 2, d // 8 + 2 * (d % 4)])
    turned[...] = jnp.transpose(jnp.concatenate(stack, axis=0))
    both_out[0] = turned[pl.ds(pl.multiple_of(core * CHUNK, CHUNK), CHUNK), :]
    for copy in copies:
        copy.wait_recv()
    wide = lax.dot_general(
        mine_cut[...],
        jnp.concatenate(cut_in_two(total[...].reshape(NZ, MODES)), axis=0),
        (((1,), (1,)), ((), ())),
        preferred_element_type=jnp.float32,
    )
    wide = four_sums(wide, CHUNK)
    smooth = jnp.dot(
        jnp.concatenate(cut_in_two(wide), axis=0),
        z_cut[...],
        preferred_element_type=jnp.float32,
    )
    both_out[1] = four_sums(smooth, CHUNK)
    for copy in copies:
        copy.wait_send()


def on_device(
    courant,
    source_states,
    adjoint_states,
    strips,
    aperture,
    source_cell,
    wavelet,
    receiver_cells,
    residuals,
):
    table = operator_table()
    vmem = pl.BlockSpec(memory_space=pltpu.VMEM)
    hbm = pl.BlockSpec(memory_space=pltpu.HBM)
    smem = pl.BlockSpec(memory_space=pltpu.SMEM)
    f32 = jnp.float32
    dma = pltpu.SemaphoreType.DMA
    others = SHOTS - 1
    state = pltpu.VMEM((ROWS + 16, NZ), f32)
    field = pltpu.VMEM((ROWS, NZ), f32)
    both = pl.pallas_call(
        kernel,
        out_shape=jax.ShapeDtypeStruct((2, CHUNK, NZ), f32),
        in_specs=[smem] * 4 + [hbm] * 7,
        out_specs=vmem,
        scratch_shapes=[
            pltpu.VMEM((NY, NZ), f32),
            pltpu.VMEM((2, NY, NZ), f32),
            pltpu.VMEM((2, NY, NZ), f32),
            pltpu.VMEM((STEPS, 2, 2, NZ), f32),
            pltpu.VMEM((2, NREC), jnp.int32),
            pltpu.VMEM((STEPS, 1, NREC), f32),
            pltpu.VMEM(table.shape, f32),
            state,
            state,
            state,
            state,
            field,
            field,
            pltpu.VMEM((2, ROWS, NZ), f32),
            pltpu.VMEM((4, ROWS, NZ), f32),
            pltpu.VMEM((4, ROWS, NZ), f32),
            field,
            pltpu.VMEM((ROWS + 4 * TILE, NZ), f32),
            pltpu.VMEM((NZ, ROWS), f32),
            pltpu.VMEM((NZ, ROWS), f32),
            pltpu.VMEM((NZ, ROWS), f32),
            pltpu.VMEM((NZ, ROWS), f32),
            pltpu.VMEM((NZ, ROWS + 4 * TILE), f32),
            pltpu.VMEM((QUARTERS, 4, 8, NY), f32),
            pltpu.VMEM((QUARTERS, 4, 8, NY), f32),
            pltpu.VMEM((2, 4, 8, NY), f32),
            pltpu.VMEM((2, 4, 8, NY), f32),
            pltpu.VMEM((2, 4, 8, NY), f32),
            pltpu.VMEM((2, 4, 8, NY), f32),
            pltpu.VMEM((LAYERS, 8, NY), f32),
            pltpu.VMEM((LAYERS, 8, NY), f32),
            pltpu.VMEM((LAYERS, 8, TILE), f32),
            pltpu.VMEM((2, LAYERS, 8, TILE), f32),
            pltpu.VMEM((TILE, NZ), f32),
            pltpu.VMEM((8, NZ), f32),
            pltpu.VMEM((others, 8, NZ), f32),
            pltpu.VMEM((2, LAYERS, 8, NZ), f32),
            pltpu.VMEM((NY, 2 * MODES), jnp.bfloat16),
            pltpu.VMEM((2 * CHUNK, MODES), jnp.bfloat16),
            pltpu.VMEM((NZ, 2 * NZ), jnp.bfloat16),
            pltpu.SemaphoreType.REGULAR((5,)),
            dma((8,)),
            dma((QUARTERS, 2)),
            dma((QUARTERS, 2)),
            dma((4, 2)),
            dma((4, 2)),
            dma((2, QUARTERS)),
            dma((2, QUARTERS)),
            dma((2, LAYERS)),
            dma((2, LAYERS)),
            dma((LAYERS,)),
            dma((LAYERS,)),
            dma((others,)),
            dma((others,)),
            dma((others,)),
            dma((others,)),
        ],
        compiler_params=pltpu.CompilerParams(
            collective_id=0, has_side_effects=True, vmem_limit_bytes=63 << 20
        ),
        name="inversion",
    )(
        aperture,
        source_cell,
        wavelet,
        jnp.asarray(gauss_table(PLANES, float(PLANES) / 4.0)),
        courant[0],
        source_states[0, :, 0],
        adjoint_states[0, :, 0],
        strips[0, :, :, 0],
        receiver_cells[0].T,
        residuals.transpose(1, 0, 2),
        jnp.asarray(table),
    )
    return (both[0:1], both[1:2])


def solution(mesh):
    placed = (
        P("pen", None, None),
        P("shot", None, "pen", None, None),
        P("shot", None, "pen", None, None),
        P("shot", None, None, "pen", None, None),
        P("shot", None),
        P("shot", None),
        P("shot", None),
        P("shot", None, None),
        P("shot", None, None),
    )
    return jax.shard_map(
        on_device,
        mesh=mesh,
        in_specs=placed,
        out_specs=(P("pen", "shot", None), P("pen", "shot", None)),
        check_vma=False,
    )
```

```python
import math

import jax
import jax.numpy as jnp
import numpy as np
from jax import lax
from jax.experimental import pallas as pl
from jax.experimental.pallas import tpu as pltpu
from jax.sharding import PartitionSpec as P

TILE = 128
NY = 1024
NZ = 128
AMAX = 6
STEPS = 3
NREC = 512
SHOTS = 16
PLANES = 16
ROWS = AMAX * TILE
CHUNK = NY // SHOTS
MODES = 128
DEPTH = 2
SHIFTS = NY // TILE - AMAX + 1
QUARTERS = 4
DEEP = NZ // QUARTERS
DAMPING = 1.0
SIGMA_Z = 4.0
MESH = pl.DeviceIdType.MESH
HIGHEST = lax.Precision.HIGHEST
LAYERS = 8
SIDE = 4


def hops(*steps):
    return -sum(min(step, size - step) for step, size in steps)


PEN_REL = sorted(
    [(dy, dx) for dy in range(SIDE) for dx in range(SIDE) if (dy, dx) != (0, 0)],
    key=lambda rel: hops((rel[0], SIDE), (rel[1], SIDE)),
)

SHOT_REL = sorted(
    [(dz, dc) for dz in range(LAYERS) for dc in range(2) if (dz, dc) != (0, 0)],
    key=lambda rel: hops((rel[0], LAYERS), (rel[1], 2)),
)


def wave_table(length, spread):
    half = MODES // 2
    order = np.concatenate([np.arange(half), np.arange(1, half + 1)])
    angle = 2.0 * np.pi * ((order[:, None] * np.arange(length)[None, :]) % length) / length
    waves = np.where(np.arange(2 * half)[:, None] < half, np.cos(angle), np.sin(angle))
    weights = np.exp(-0.5 * (spread * 2.0 * np.pi * order / length) ** 2) / length
    weights = np.where(order == 0, weights, 2.0 * weights)
    return waves.T, weights


def circulant_table(length, spread):
    frequency = np.fft.fftfreq(length)
    weights = np.exp(-0.5 * (spread * 2.0 * np.pi * frequency) ** 2)
    vector = np.real(np.fft.ifft(weights))
    position = np.arange(length)
    return vector[(position[:, None] - position[None, :]) % length].astype(np.float32)


def gauss_table(total, spread):
    position = np.arange(total)
    distance = (position[:, None] - position[None, :]).astype(np.float64)
    table = np.exp(-0.5 * (distance / spread) ** 2) / (spread * math.sqrt(2.0 * math.pi))
    return table.astype(np.float32)


def depth_slot(layer, core):
    return 8 * (layer % 2) + 4 * core + layer // 2


def operator_table():
    waves, weights = wave_table(NY, float(NY) / float(SHOTS))
    owners = [(core, layer) for core in range(2) for layer in range(LAYERS)]
    depths = [8 * depth_slot(layer, core) + i for core, layer in owners for i in range(8)]
    z_part = circulant_table(NZ, SIGMA_Z)[np.array(depths)]
    return np.concatenate([waves, z_part, np.tile(weights, (8, 1))]).astype(np.float32)


def cut_in_two(value):
    coarse = value.astype(jnp.bfloat16)
    return coarse, (value - coarse.astype(jnp.float32)).astype(jnp.bfloat16)


def four_sums(out, rows):
    first = out[:rows, :NZ] + (out[:rows, NZ:] + out[rows:, :NZ])
    return first + out[rows:, NZ:]


def block_rows(b, pad=0):
    return pl.ds(pl.multiple_of(b * TILE + pad, 8), TILE)


def kernel(
    aperture,
    source_cell,
    wavelet,
    gauss,
    courant_hbm,
    source_hbm,
    adjoint_hbm,
    strips_hbm,
    cells_hbm,
    residuals_hbm,
    table_hbm,
    both_out,
    courant,
    source,
    adjoint,
    strips,
    cells,
    residuals,
    table,
    ua,
    ub,
    ra,
    rb,
    cw,
    hit,
    inj,
    from_low,
    from_high,
    grad,
    light,
    turned_u,
    low_turned,
    high_turned,
    slope,
    whole,
    split_g,
    split_l,
    pair_g,
    pair_l,
    mine_g,
    mine_l,
    ring_g,
    ring_l,
    tiles,
    tiles_in,
    turned,
    coef,
    coef_in,
    total,
    waves_cut,
    mine_cut,
    z_cut,
    known,
    load_sem,
    last_send,
    last_recv,
    halo_send,
    halo_recv,
    pair_send,
    pair_recv,
    ring_send,
    ring_recv,
    tiles_send,
    tiles_recv,
    coef_send,
    coef_recv,
    total_send,
    total_recv,
):
    shot = lax.axis_index("shot")
    pen = lax.axis_index("pen")
    z, core = shot // 2, lax.rem(shot, 2)
    py, px = pen // SIDE, lax.rem(pen, SIDE)

    def pen_peer(rel):
        dy, dx = rel
        return (shot, lax.rem(py + dy, SIDE) * SIDE + lax.rem(px + dx, SIDE))

    loads = []
    for i, (origin, place) in enumerate(
        (
            (source_hbm.at[0], source.at[0]),
            (source_hbm.at[1], source.at[1]),
            (adjoint_hbm, adjoint),
            (courant_hbm, courant),
            (cells_hbm, cells),
            (residuals_hbm, residuals),
            (strips_hbm, strips),
            (table_hbm, table),
        )
    ):
        loads.append(pltpu.make_async_copy(origin, place, load_sem.at[i]))
    loads[0].start()

    barrier = pltpu.get_barrier_semaphore()
    def pen_at(offset):
        return (shot, lax.rem(pen + offset, PLANES))

    def shot_at(dz, dc):
        return (lax.rem(z + dz, LAYERS) * 2 + lax.rem(core + dc, 2), pen)

    near_pen = [pen_at(o) for o in (1, PLANES - 1, SIDE, PLANES - SIDE)]
    near_shot = [shot_at(1, 0), shot_at(LAYERS - 1, 0), shot_at(0, 1)]
    for peer in near_pen + near_shot:
        pl.semaphore_signal(barrier, inc=1, device_id=peer, device_id_type=MESH)

    for load in loads[1:]:
        load.start()

    greetings = [
        (0, near_pen),
        (1, near_shot),
        (2, [pen_at(SIDE), pen_at(PLANES - SIDE)]),
        (3, [shot_at(2, 0), shot_at(LAYERS - 2, 0)]),
        (4, [shot_at(0, 1)]),
    ]

    def greet(k):
        for peer in greetings[k][1]:
            pl.semaphore_signal(known.at[k], inc=1, device_id=peer, device_id_type=MESH)

    def greeted(k):
        pl.semaphore_wait(known.at[k], len(greetings[k][1]))

    first = aperture[0, 0]
    count = aperture[0, 1]
    window = jnp.minimum(first, NY // TILE - AMAX)
    low = first - window
    high = low + count
    start = window * TILE

    edge = jnp.zeros((8, NZ), jnp.float32)
    for ref in (ua, ub, ra, rb):
        ref[pl.ds(0, 8), :] = edge
        ref[pl.ds(ROWS + 8, 8), :] = edge

    lane = lax.broadcasted_iota(jnp.int32, (TILE, NZ), 1)
    row = lax.broadcasted_iota(jnp.int32, (TILE, NZ), 0)

    def pick(options, like):
        where_from = like * 0 + window
        out = options[SHIFTS - 1]
        for i in range(SHIFTS - 2, -1, -1):
            out = jnp.where(where_from == i, options[i], out)
        return out

    def take_window(b, places):
        row_here = row + b * TILE
        inside = (row_here >= low * TILE) & (row_here < high * TILE)
        for ref, lead, out, pad in places:
            options = [ref[(*lead, block_rows(b, i * TILE))] for i in range(SHIFTS)]
            out[block_rows(b, pad), :] = jnp.where(inside, pick(options, row), 0.0)

    def load_block(places):
        def body(b, carry):
            take_window(b, places)
            return carry

        lax.fori_loop(0, AMAX, body, 0)

    loads[0].wait()
    load_block([(source, (0,), ua, 8)])

    pl.semaphore_wait(barrier, len(near_pen) + len(near_shot))

    up, down = near_pen[0], near_pen[1]

    def exchange(body, low, high, send, recv):
        upward = pltpu.make_async_remote_copy(
            body, low, send.at[0], recv.at[0], device_id=up, device_id_type=MESH
        )
        downward = pltpu.make_async_remote_copy(
            body, high, send.at[1], recv.at[1], device_id=down, device_id_type=MESH
        )

        class Pair:
            def start(self):
                pl.when(pen < PLANES - 1)(upward.start)
                pl.when(pen > 0)(downward.start)

            def sent(self):
                pl.when(pen < PLANES - 1)(upward.wait_send)
                pl.when(pen > 0)(downward.wait_send)

            def arrived(self):
                pl.when(pen > 0)(upward.wait_recv)
                pl.when(pen < PLANES - 1)(downward.wait_recv)

        return Pair()

    def halo(state, slot):
        half = ROWS // 2
        return [
            exchange(
                state.at[pl.ds(8 + i * half, half), :],
                from_low.at[slot, pl.ds(i * half, half), :],
                from_high.at[slot, pl.ds(i * half, half), :],
                halo_send.at[slot, i],
                halo_recv.at[slot, i],
            )
            for i in range(2)
        ]

    def arrived(pair):
        for part in pair:
            part.arrived()

    def follow(before, after):
        for i in range(2):
            before[i].sent()
            after[i].start()

    def halo_turned(k):
        at = pl.ds(k * DEEP, DEEP)
        return exchange(
            turned_u.at[at, :],
            low_turned.at[at, :],
            high_turned.at[at, :],
            last_send.at[k],
            last_recv.at[k],
        )

    not_first = lane > 0
    not_last = lane < NZ - 1

    def laplace(state, slot, b):
        wide = state[pl.ds(pl.multiple_of(b * TILE, TILE), TILE + 16), :]
        here = wide[8 : TILE + 8]
        at = block_rows(b)
        beside = pltpu.roll(wide, 1, 0)[8 : TILE + 8]
        beside = beside + pltpu.roll(wide, TILE + 15, 0)[8 : TILE + 8]
        beside = beside + jnp.where(not_first, pltpu.roll(here, 1, 1), 0.0)
        beside = beside + jnp.where(not_last, pltpu.roll(here, NZ - 1, 1), 0.0)
        if slot is not None:
            beside = beside + (from_low[slot, at, :] + from_high[slot, at, :])
        return here, beside - 6.0 * here

    def with_strips(b, moment, new):
        row_here = row + b * TILE
        for i in range(2):
            new = jnp.where(
                row_here == low * TILE + i, strips[moment, 0, pl.ds(i, 1), :], new
            )
            new = jnp.where(
                row_here == high * TILE - 2 + i, strips[moment, 1, pl.ds(i, 1), :], new
            )
        return new

    def columns(b, pad=0):
        return pl.ds(pl.multiple_of(b * TILE + pad, TILE), TILE)

    def source_step(now, old, slot, moment, adjoint_now):
        amplitude = wavelet[0, moment]

        def body(b, carry):
            here, lap = laplace(now, slot, b)
            at = block_rows(b)
            at8 = block_rows(b, 8)
            before = old[at8, :]
            new = 2.0 * here - before + cw[at, :] * (lap + amplitude * hit[at, :])
            new = with_strips(b, moment, new)
            at256 = block_rows(b, 2 * TILE)
            step = (before - 2.0 * here + new) * adjoint_now[at8, :]
            old[at8, :] = new
            if moment == 0:
                grad[at, :] = step
                light[at256, :] = here * here
            else:
                grad[at, :] = grad[at, :] + step
                light[at256, :] = light[at256, :] + here * here + new * new
                turned_u[:, columns(b)] = jnp.transpose(new)
            return carry

        lax.fori_loop(0, AMAX, body, 0)

    def last_step(now, old, moment, adjoint_now):
        amplitude = wavelet[0, moment]

        def body(b, carry):
            here, lap = laplace(now, None, b)
            at = block_rows(b)
            at8 = block_rows(b, 8)
            before = old[at8, :]
            new = 2.0 * here - before + cw[at, :] * (lap + amplitude * hit[at, :])
            new = with_strips(b, moment, new)
            free = cw[at, :]
            row_here = row + b * TILE
            for i in range(2):
                free = jnp.where(row_here == low * TILE + i, 0.0, free)
                free = jnp.where(row_here == high * TILE - 2 + i, 0.0, free)
            ahead = adjoint_now[at8, :]
            known_part = grad[at, :] + (before - 2.0 * here + new) * ahead
            whole[:, columns(b, 2 * TILE)] = jnp.transpose(known_part)
            slope[:, columns(b)] = jnp.transpose(free * ahead)
            return carry

        lax.fori_loop(0, AMAX, body, 0)

    def adjoint_step(now, old, slot, moment):
        def body(b, carry):
            here, lap = laplace(now, slot, b)
            at = block_rows(b)
            at8 = block_rows(b, 8)
            old[at8, :] = 2.0 * here - old[at8, :] + cw[at, :] * (lap + inj[moment, at, :])
            return carry

        lax.fori_loop(0, AMAX, body, 0)

    u0, r0, u1, r1 = halo(ua, 0), halo(ra, 1), halo(ub, 2), halo(rb, 3)
    u2 = [halo_turned(k) for k in range(QUARTERS)]
    u0[0].start()
    greet(0)
    greet(1)
    loads[1].wait()
    load_block([(source, (1,), ub, 8)])
    u0[1].start()

    @pl.when(pen == 0)
    def _():
        from_low[...] = jnp.zeros_like(from_low)
        low_turned[...] = jnp.zeros_like(low_turned)

    @pl.when(pen == PLANES - 1)
    def _():
        from_high[...] = jnp.zeros_like(from_high)
        high_turned[...] = jnp.zeros_like(high_turned)

    loads[2].wait()
    load_block([(adjoint, (0,), ra, 8), (adjoint, (1,), rb, 8)])
    follow(u0, r0)
    for load in loads[3:]:
        load.wait()
    greeted(0)
    greeted(1)
    greet(2)
    greet(3)
    load_block([(courant, (), cw, 0)])

    cell_row = jnp.where(cells[pl.ds(0, 1), :] == pen, cells[pl.ds(1, 1), :] - start, -1)
    slab = lax.broadcasted_iota(jnp.int32, (8, NREC), 0)
    values = jnp.where(lax.rem(slab, 2) == 0, residuals[0], residuals[1])
    coarse = values.astype(jnp.bfloat16).astype(jnp.float32)
    middle = (values - coarse).astype(jnp.bfloat16).astype(jnp.float32)
    fine = values - coarse - middle
    values = jnp.where(slab < DEPTH + 2, coarse, jnp.where(slab < DEPTH + 4, middle, fine))
    values = jnp.where(slab < DEPTH, 0.0, values)
    values = jnp.concatenate([values, jnp.zeros((NZ - 8, NREC), jnp.float32)], axis=0)
    values = jnp.transpose(values).astype(jnp.bfloat16)
    rows_wide = lax.broadcasted_iota(jnp.int32, (TILE, NREC), 0)

    def inject_block(b, carry):
        chosen = jnp.where(rows_wide == cell_row - b * TILE, 1.0, 0.0).astype(jnp.bfloat16)
        out = jnp.dot(chosen, values, preferred_element_type=jnp.float32)
        out = out + pltpu.roll(out, NZ - 2, 1) + pltpu.roll(out, NZ - 4, 1)
        at = block_rows(b)
        inj[0, at, :] = jnp.where(lane == DEPTH, out, 0.0)
        inj[1, at, :] = jnp.where(lane == DEPTH, pltpu.roll(out, NZ - 1, 1), 0.0)
        key = row + (b * TILE + pen * NY)
        cell = source_cell[0, 0] * NY + source_cell[0, 1] - start
        here = (key == cell) & (lane == source_cell[0, 2])
        hit[at, :] = jnp.where(here, 1.0, 0.0)
        return carry

    lax.fori_loop(0, AMAX, inject_block, 0)
    light[pl.ds(0, 2 * TILE), :] = jnp.zeros((2 * TILE, NZ), jnp.float32)
    light[pl.ds(ROWS + 2 * TILE, 2 * TILE), :] = jnp.zeros((2 * TILE, NZ), jnp.float32)
    whole[:, pl.ds(0, 2 * TILE)] = jnp.zeros((NZ, 2 * TILE), jnp.float32)
    whole[:, pl.ds(ROWS + 2 * TILE, 2 * TILE)] = jnp.zeros((NZ, 2 * TILE), jnp.float32)
    greeted(2)
    greeted(3)
    greet(4)

    def spread_light():
        def body(g, carry):
            options = []
            for shift in range(SHIFTS):
                options.append(light[block_rows(g, (SHIFTS - 1 - shift) * TILE), :])
            flat = jnp.transpose(pick(options, row))
            for d in range(SHOTS):
                k, j = d // 4, d % 4
                split_l[k, j, :, columns(g)] = flat[8 * d : 8 * d + 8]
            return carry

        lax.fori_loop(0, NY // TILE, body, 0)

    def spread_quarter(k):
        at = pl.ds(k * DEEP, DEEP)
        inner = pl.ds(2 * TILE, ROWS)
        pushed = low_turned[at, :] + high_turned[at, :]
        whole[at, inner] = whole[at, inner] + slope[at, :] * pushed
        for j in range(4):
            rows8 = pl.ds(k * DEEP + 8 * j, 8)
            options = []
            for shift in range(SHIFTS):
                options.append(whole[rows8, pl.ds((SHIFTS - 1 - shift) * TILE, NY)])
            like = lax.broadcasted_iota(jnp.int32, (8, NY), 0)
            split_g[k, j] = pick(options, like)

    class Sum:
        def __init__(self, split, pair, mine, ring, which):
            self.split, self.pair, self.mine, self.ring = split, pair, mine, ring
            self.pairs, self.targets = [], []
            for k in range(QUARTERS):
                self.pairs.append(
                    pltpu.make_async_remote_copy(
                        split.at[k], pair.at[k // 2], pair_send.at[which, k],
                        pair_recv.at[which, k],
                        device_id=shot_at(0, 1), device_id_type=MESH,
                    )
                )
                for j in range(4):
                    target = k // 2 + 2 * j
                    slot = lax.rem(target - z + 2 * LAYERS - 1, LAYERS)
                    copy = pltpu.make_async_remote_copy(
                        mine.at[k // 2, j], ring.at[slot], ring_send.at[which, target],
                        ring_recv.at[which, slot],
                        device_id=(2 * target + k % 2, pen), device_id_type=MESH,
                    )
                    self.targets.append(((core == k % 2) & (z != target), copy))
            self.arrivals = [
                pltpu.make_async_remote_copy(
                    mine.at[0, 0], ring.at[slot], ring_send.at[which, 0],
                    ring_recv.at[which, slot],
                    device_id=shot_at(1, 0), device_id_type=MESH,
                )
                for slot in range(LAYERS - 1)
            ]

        def start_pair(self, k):
            pl.when(core != k % 2)(self.pairs[k].start)

        def start_ring(self, k):
            @pl.when(core == k % 2)
            def _():
                self.pairs[k].wait_recv()
                self.mine[k // 2] = self.split[k] + self.pair[k // 2]

            for there, copy in self.targets[4 * k : 4 * k + 4]:
                pl.when(there)(copy.start)

        def finish(self):
            total_here = self.mine[lax.rem(z, 2), z // 2]
            for slot in range(LAYERS - 1):
                self.arrivals[slot].wait_recv()
                total_here = total_here + self.ring[slot]
            for there, copy in self.targets:
                pl.when(there)(copy.wait_send)
            for k in range(QUARTERS):
                pl.when(core != k % 2)(self.pairs[k].wait_send)
            return total_here

    sum_l = Sum(split_l, pair_l, mine_l, ring_l, 0)
    sum_g = Sum(split_g, pair_g, mine_g, ring_g, 1)

    arrived(u0)
    source_step(ua, ub, 0, 0, ra)
    follow(r0, u1)
    greeted(4)
    arrived(r0)
    adjoint_step(ra, rb, 1, 0)
    follow(u1, r1)

    def cut_block(g, carry):
        at = block_rows(g)
        waves_cut[at, :] = jnp.concatenate(cut_in_two(table[at, :]), axis=1)
        return carry

    lax.fori_loop(0, NY // TILE, cut_block, 0)
    z_cut[...] = jnp.concatenate(cut_in_two(table[pl.ds(NY, NZ), :]), axis=1)
    rows_here = pl.ds(pl.multiple_of(shot * CHUNK, CHUNK), CHUNK)
    mine_cut[...] = jnp.concatenate(cut_in_two(table[rows_here, :]), axis=0)
    arrived(u1)
    source_step(ub, ua, 2, 1, rb)
    spread_light()
    for k in range(QUARTERS):
        sum_l.start_pair(k)
    for k in range(QUARTERS):
        sum_l.start_ring(k)
    follow(r1, u2)
    arrived(r1)
    adjoint_step(rb, ra, 3, 1)
    u2[0].sent()
    u2[2].start()
    last_step(ua, ub, 2, ra)
    u2[1].sent()
    u2[3].start()
    for k in range(QUARTERS):
        u2[k].arrived()
        spread_quarter(k)
        sum_g.start_pair(k)
        if k > 0:
            sum_g.start_ring(k - 1)
    sum_g.start_ring(QUARTERS - 1)
    for k in range(2, QUARTERS):
        u2[k].sent()
    lighting = sum_l.finish()
    gradient = sum_g.finish()
    precond = gradient / (lighting + DAMPING)
    for h in range(LAYERS):
        tiles[h] = precond[:, h * TILE : (h + 1) * TILE]

    def over_layers(origin, place, send, recv):
        copies = []
        for i, d in enumerate((4, 3, 5, 2, 6, 1, 7)):
            copies.append(
                pltpu.make_async_remote_copy(
                    origin(lax.rem(z + d, LAYERS)), place.at[core, z], send.at[i], recv.at[i],
                    device_id=shot_at(d, 0), device_id_type=MESH,
                )
            )
        return copies

    def to_partner(place, send, recv):
        return pltpu.make_async_remote_copy(
            place.at[core], place.at[core], send.at[LAYERS - 1], recv.at[LAYERS - 1],
            device_id=shot_at(0, 1), device_id_type=MESH,
        )

    tile_copies = over_layers(lambda layer: tiles.at[layer], tiles_in, tiles_send, tiles_recv)
    tile_pair = to_partner(tiles_in, tiles_send, tiles_recv)
    tally = jnp.dot(
        jnp.concatenate(cut_in_two(precond), axis=0),
        waves_cut[...],
        preferred_element_type=jnp.float32,
    )
    tally = four_sums(tally, 8)
    coef[...] = tally
    copies = []
    for i, rel in enumerate(PEN_REL):
        copies.append(
            pltpu.make_async_remote_copy(
                coef, coef_in.at[i], coef_send.at[i], coef_recv.at[i],
                device_id=pen_peer(rel), device_id_type=MESH,
            )
        )
    for copy in copies:
        copy.start()
    for copy in tile_copies:
        copy.start()
    tiles_in[core, z] = tiles[z]
    mixed = tally * gauss[pen, pen]
    for i, (dy, dx) in enumerate(PEN_REL):
        copies[i].wait_recv()
        origin = lax.rem(py + SIDE - dy, SIDE) * SIDE + lax.rem(px + SIDE - dx, SIDE)
        mixed = mixed + coef_in[i] * gauss[pen, origin]
    coef_copies = copies
    total[core, z] = mixed * table[pl.ds(NY + NZ, 8), :]
    copies = []
    for i, (dz, dc) in enumerate(SHOT_REL):
        copies.append(
            pltpu.make_async_remote_copy(
                total.at[core, z], total.at[core, z], total_send.at[i], total_recv.at[i],
                device_id=shot_at(dz, dc), device_id_type=MESH,
            )
        )
    for copy in copies:
        copy.start()
    for copy in tile_copies:
        copy.wait_recv()
    tile_pair.start()
    for copy in coef_copies + tile_copies:
        copy.wait_send()
    tile_pair.wait()
    stack = []
    for d in range(SHOTS):
        stack.append(tiles_in[(d // 4) % 2, d // 8 + 2 * (d % 4)])
    turned[...] = jnp.transpose(jnp.concatenate(stack, axis=0))
    both_out[0] = turned[pl.ds(pl.multiple_of(core * CHUNK, CHUNK), CHUNK), :]
    for copy in copies:
        copy.wait_recv()
    wide = lax.dot_general(
        mine_cut[...],
        jnp.concatenate(cut_in_two(total[...].reshape(NZ, MODES)), axis=0),
        (((1,), (1,)), ((), ())),
        preferred_element_type=jnp.float32,
    )
    wide = four_sums(wide, CHUNK)
    smooth = jnp.dot(
        jnp.concatenate(cut_in_two(wide), axis=0),
        z_cut[...],
        preferred_element_type=jnp.float32,
    )
    both_out[1] = four_sums(smooth, CHUNK)
    for copy in copies:
        copy.wait_send()


def on_device(
    courant,
    source_states,
    adjoint_states,
    strips,
    aperture,
    source_cell,
    wavelet,
    receiver_cells,
    residuals,
):
    table = operator_table()
    vmem = pl.BlockSpec(memory_space=pltpu.VMEM)
    hbm = pl.BlockSpec(memory_space=pltpu.HBM)
    smem = pl.BlockSpec(memory_space=pltpu.SMEM)
    f32 = jnp.float32
    dma = pltpu.SemaphoreType.DMA
    others = SHOTS - 1
    state = pltpu.VMEM((ROWS + 16, NZ), f32)
    field = pltpu.VMEM((ROWS, NZ), f32)
    both = pl.pallas_call(
        kernel,
        out_shape=jax.ShapeDtypeStruct((2, CHUNK, NZ), f32),
        in_specs=[smem] * 4 + [hbm] * 7,
        out_specs=vmem,
        scratch_shapes=[
            pltpu.VMEM((NY, NZ), f32),
            pltpu.VMEM((2, NY, NZ), f32),
            pltpu.VMEM((2, NY, NZ), f32),
            pltpu.VMEM((STEPS, 2, 2, NZ), f32),
            pltpu.VMEM((2, NREC), jnp.int32),
            pltpu.VMEM((STEPS, 1, NREC), f32),
            pltpu.VMEM(table.shape, f32),
            state,
            state,
            state,
            state,
            field,
            field,
            pltpu.VMEM((2, ROWS, NZ), f32),
            pltpu.VMEM((4, ROWS, NZ), f32),
            pltpu.VMEM((4, ROWS, NZ), f32),
            field,
            pltpu.VMEM((ROWS + 4 * TILE, NZ), f32),
            pltpu.VMEM((NZ, ROWS), f32),
            pltpu.VMEM((NZ, ROWS), f32),
            pltpu.VMEM((NZ, ROWS), f32),
            pltpu.VMEM((NZ, ROWS), f32),
            pltpu.VMEM((NZ, ROWS + 4 * TILE), f32),
            pltpu.VMEM((QUARTERS, 4, 8, NY), f32),
            pltpu.VMEM((QUARTERS, 4, 8, NY), f32),
            pltpu.VMEM((2, 4, 8, NY), f32),
            pltpu.VMEM((2, 4, 8, NY), f32),
            pltpu.VMEM((2, 4, 8, NY), f32),
            pltpu.VMEM((2, 4, 8, NY), f32),
            pltpu.VMEM((LAYERS, 8, NY), f32),
            pltpu.VMEM((LAYERS, 8, NY), f32),
            pltpu.VMEM((LAYERS, 8, TILE), f32),
            pltpu.VMEM((2, LAYERS, 8, TILE), f32),
            pltpu.VMEM((TILE, NZ), f32),
            pltpu.VMEM((8, NZ), f32),
            pltpu.VMEM((others, 8, NZ), f32),
            pltpu.VMEM((2, LAYERS, 8, NZ), f32),
            pltpu.VMEM((NY, 2 * MODES), jnp.bfloat16),
            pltpu.VMEM((2 * CHUNK, MODES), jnp.bfloat16),
            pltpu.VMEM((NZ, 2 * NZ), jnp.bfloat16),
            pltpu.SemaphoreType.REGULAR((5,)),
            dma((8,)),
            dma((QUARTERS, 2)),
            dma((QUARTERS, 2)),
            dma((4, 2, 2)),
            dma((4, 2, 2)),
            dma((2, QUARTERS)),
            dma((2, QUARTERS)),
            dma((2, LAYERS)),
            dma((2, LAYERS)),
            dma((LAYERS,)),
            dma((LAYERS,)),
            dma((others,)),
            dma((others,)),
            dma((others,)),
            dma((others,)),
        ],
        compiler_params=pltpu.CompilerParams(
            collective_id=0, has_side_effects=True, vmem_limit_bytes=63 << 20
        ),
        name="inversion",
    )(
        aperture,
        source_cell,
        wavelet,
        jnp.asarray(gauss_table(PLANES, float(PLANES) / 4.0)),
        courant[0],
        source_states[0, :, 0],
        adjoint_states[0, :, 0],
        strips[0, :, :, 0],
        receiver_cells[0].T,
        residuals.transpose(1, 0, 2),
        jnp.asarray(table),
    )
    return (both[0:1], both[1:2])


def solution(mesh):
    placed = (
        P("pen", None, None),
        P("shot", None, "pen", None, None),
        P("shot", None, "pen", None, None),
        P("shot", None, None, "pen", None, None),
        P("shot", None),
        P("shot", None),
        P("shot", None),
        P("shot", None, None),
        P("shot", None, None),
    )
    return jax.shard_map(
        on_device,
        mesh=mesh,
        in_specs=placed,
        out_specs=(P("pen", "shot", None), P("pen", "shot", None)),
        check_vma=False,
    )
```

```python
import math

import jax
import jax.numpy as jnp
import numpy as np
from jax import lax
from jax.experimental import pallas as pl
from jax.experimental.pallas import tpu as pltpu
from jax.sharding import PartitionSpec as P

TILE = 128
NY = 1024
NZ = 128
AMAX = 6
STEPS = 3
NREC = 512
SHOTS = 16
PLANES = 16
ROWS = AMAX * TILE
CHUNK = NY // SHOTS
MODES = 128
DEPTH = 2
SHIFTS = NY // TILE - AMAX + 1
QUARTERS = 4
DEEP = NZ // QUARTERS
DAMPING = 1.0
SIGMA_Z = 4.0
MESH = pl.DeviceIdType.MESH
HIGHEST = lax.Precision.HIGHEST
LAYERS = 8
SIDE = 4


def hops(*steps):
    return -sum(min(step, size - step) for step, size in steps)


PEN_REL = sorted(
    [(dy, dx) for dy in range(SIDE) for dx in range(SIDE) if (dy, dx) != (0, 0)],
    key=lambda rel: hops((rel[0], SIDE), (rel[1], SIDE)),
)

SHOT_REL = sorted(
    [(dz, dc) for dz in range(LAYERS) for dc in range(2) if (dz, dc) != (0, 0)],
    key=lambda rel: hops((rel[0], LAYERS), (rel[1], 2)),
)


def wave_table(length, spread):
    half = MODES // 2
    order = np.concatenate([np.arange(half), np.arange(1, half + 1)])
    angle = 2.0 * np.pi * ((order[:, None] * np.arange(length)[None, :]) % length) / length
    waves = np.where(np.arange(2 * half)[:, None] < half, np.cos(angle), np.sin(angle))
    weights = np.exp(-0.5 * (spread * 2.0 * np.pi * order / length) ** 2) / length
    weights = np.where(order == 0, weights, 2.0 * weights)
    return waves.T, weights


def circulant_table(length, spread):
    frequency = np.fft.fftfreq(length)
    weights = np.exp(-0.5 * (spread * 2.0 * np.pi * frequency) ** 2)
    vector = np.real(np.fft.ifft(weights))
    position = np.arange(length)
    return vector[(position[:, None] - position[None, :]) % length].astype(np.float32)


def gauss_table(total, spread):
    position = np.arange(total)
    distance = (position[:, None] - position[None, :]).astype(np.float64)
    table = np.exp(-0.5 * (distance / spread) ** 2) / (spread * math.sqrt(2.0 * math.pi))
    return table.astype(np.float32)


def depth_slot(layer, core):
    return 8 * (layer % 2) + 4 * core + layer // 2


def operator_table():
    waves, weights = wave_table(NY, float(NY) / float(SHOTS))
    owners = [(core, layer) for core in range(2) for layer in range(LAYERS)]
    depths = [8 * depth_slot(layer, core) + i for core, layer in owners for i in range(8)]
    z_part = circulant_table(NZ, SIGMA_Z)[np.array(depths)]
    x_part = np.repeat(gauss_table(PLANES, float(PLANES) / 4.0).reshape(-1, 1), NZ, axis=1)
    pieces = [waves, z_part, np.tile(weights, (8, 1)), x_part]
    return np.concatenate(pieces).astype(np.float32)


def cut_in_two(value):
    coarse = value.astype(jnp.bfloat16)
    return coarse, (value - coarse.astype(jnp.float32)).astype(jnp.bfloat16)


def four_sums(out, rows):
    first = out[:rows, :NZ] + (out[:rows, NZ:] + out[rows:, :NZ])
    return first + out[rows:, NZ:]


def block_rows(b, pad=0):
    return pl.ds(pl.multiple_of(b * TILE + pad, 8), TILE)


def kernel(
    aperture,
    source_cell,
    wavelet,
    courant_hbm,
    source_hbm,
    adjoint_hbm,
    strips_hbm,
    cells_hbm,
    residuals_hbm,
    table_hbm,
    both_out,
    courant,
    source,
    adjoint,
    strips,
    cells,
    residuals,
    table,
    ua,
    ub,
    ra,
    rb,
    cw,
    hit,
    inj,
    from_low,
    from_high,
    grad,
    light,
    turned_u,
    low_turned,
    high_turned,
    slope,
    whole,
    split_g,
    split_l,
    pair_g,
    pair_l,
    mine_g,
    mine_l,
    ring_g,
    ring_l,
    tiles,
    tiles_in,
    turned,
    coef,
    coef_in,
    total,
    waves_cut,
    mine_cut,
    z_cut,
    known,
    load_sem,
    last_send,
    last_recv,
    halo_send,
    halo_recv,
    pair_send,
    pair_recv,
    ring_send,
    ring_recv,
    tiles_send,
    tiles_recv,
    coef_send,
    coef_recv,
    total_send,
    total_recv,
):
    shot = lax.axis_index("shot")
    pen = lax.axis_index("pen")
    z, core = shot // 2, lax.rem(shot, 2)
    py, px = pen // SIDE, lax.rem(pen, SIDE)

    def pen_peer(rel):
        dy, dx = rel
        return (shot, lax.rem(py + dy, SIDE) * SIDE + lax.rem(px + dx, SIDE))

    loads = []
    for i, (origin, place) in enumerate(
        (
            (source_hbm.at[0], source.at[0]),
            (source_hbm.at[1], source.at[1]),
            (adjoint_hbm, adjoint),
            (courant_hbm, courant),
            (cells_hbm, cells),
            (residuals_hbm, residuals),
            (strips_hbm, strips),
            (table_hbm, table),
        )
    ):
        loads.append(pltpu.make_async_copy(origin, place, load_sem.at[i]))
    loads[0].start()

    barrier = pltpu.get_barrier_semaphore()
    def pen_at(offset):
        return (shot, lax.rem(pen + offset, PLANES))

    def shot_at(dz, dc):
        return (lax.rem(z + dz, LAYERS) * 2 + lax.rem(core + dc, 2), pen)

    near_pen = [pen_at(o) for o in (1, PLANES - 1, SIDE, PLANES - SIDE)]
    near_shot = [shot_at(1, 0), shot_at(LAYERS - 1, 0), shot_at(0, 1)]
    for peer in near_pen + near_shot:
        pl.semaphore_signal(barrier, inc=1, device_id=peer, device_id_type=MESH)

    for load in loads[1:]:
        load.start()

    greetings = [
        (0, near_pen),
        (1, near_shot),
        (2, [pen_at(SIDE), pen_at(PLANES - SIDE)]),
        (3, [shot_at(2, 0), shot_at(LAYERS - 2, 0)]),
        (4, [shot_at(0, 1)]),
    ]

    def greet(k):
        for peer in greetings[k][1]:
            pl.semaphore_signal(known.at[k], inc=1, device_id=peer, device_id_type=MESH)

    def greeted(k):
        pl.semaphore_wait(known.at[k], len(greetings[k][1]))

    first = aperture[0, 0]
    count = aperture[0, 1]
    window = jnp.minimum(first, NY // TILE - AMAX)
    low = first - window
    high = low + count
    start = window * TILE

    edge = jnp.zeros((8, NZ), jnp.float32)
    for ref in (ua, ub, ra, rb):
        ref[pl.ds(0, 8), :] = edge
        ref[pl.ds(ROWS + 8, 8), :] = edge

    lane = lax.broadcasted_iota(jnp.int32, (TILE, NZ), 1)
    row = lax.broadcasted_iota(jnp.int32, (TILE, NZ), 0)

    def pick(options, like):
        where_from = like * 0 + window
        out = options[SHIFTS - 1]
        for i in range(SHIFTS - 2, -1, -1):
            out = jnp.where(where_from == i, options[i], out)
        return out

    def take_window(b, places):
        row_here = row + b * TILE
        inside = (row_here >= low * TILE) & (row_here < high * TILE)
        for ref, lead, out, pad in places:
            options = [ref[(*lead, block_rows(b, i * TILE))] for i in range(SHIFTS)]
            out[block_rows(b, pad), :] = jnp.where(inside, pick(options, row), 0.0)

    def load_block(places):
        def body(b, carry):
            take_window(b, places)
            return carry

        lax.fori_loop(0, AMAX, body, 0)

    loads[0].wait()
    load_block([(source, (0,), ua, 8)])

    pl.semaphore_wait(barrier, len(near_pen) + len(near_shot))

    up, down = near_pen[0], near_pen[1]

    def exchange(body, low, high, send, recv):
        upward = pltpu.make_async_remote_copy(
            body, low, send.at[0], recv.at[0], device_id=up, device_id_type=MESH
        )
        downward = pltpu.make_async_remote_copy(
            body, high, send.at[1], recv.at[1], device_id=down, device_id_type=MESH
        )

        class Pair:
            def start(self):
                pl.when(pen < PLANES - 1)(upward.start)
                pl.when(pen > 0)(downward.start)

            def sent(self):
                pl.when(pen < PLANES - 1)(upward.wait_send)
                pl.when(pen > 0)(downward.wait_send)

            def arrived(self):
                pl.when(pen > 0)(upward.wait_recv)
                pl.when(pen < PLANES - 1)(downward.wait_recv)

        return Pair()

    def halo(state, slot):
        return exchange(
            state.at[pl.ds(8, ROWS), :],
            from_low.at[slot],
            from_high.at[slot],
            halo_send.at[slot],
            halo_recv.at[slot],
        )

    def halo_turned(k):
        at = pl.ds(k * DEEP, DEEP)
        return exchange(
            turned_u.at[at, :],
            low_turned.at[at, :],
            high_turned.at[at, :],
            last_send.at[k],
            last_recv.at[k],
        )

    not_first = lane > 0
    not_last = lane < NZ - 1

    def laplace(state, slot, b):
        wide = state[pl.ds(pl.multiple_of(b * TILE, TILE), TILE + 16), :]
        here = wide[8 : TILE + 8]
        at = block_rows(b)
        beside = pltpu.roll(wide, 1, 0)[8 : TILE + 8]
        beside = beside + pltpu.roll(wide, TILE + 15, 0)[8 : TILE + 8]
        beside = beside + jnp.where(not_first, pltpu.roll(here, 1, 1), 0.0)
        beside = beside + jnp.where(not_last, pltpu.roll(here, NZ - 1, 1), 0.0)
        if slot is not None:
            beside = beside + (from_low[slot, at, :] + from_high[slot, at, :])
        return here, beside - 6.0 * here

    def with_strips(b, moment, new):
        row_here = row + b * TILE
        for i in range(2):
            new = jnp.where(
                row_here == low * TILE + i, strips[moment, 0, pl.ds(i, 1), :], new
            )
            new = jnp.where(
                row_here == high * TILE - 2 + i, strips[moment, 1, pl.ds(i, 1), :], new
            )
        return new

    def columns(b, pad=0):
        return pl.ds(pl.multiple_of(b * TILE + pad, TILE), TILE)

    def source_step(now, old, slot, moment, adjoint_now):
        amplitude = wavelet[0, moment]

        def body(b, carry):
            here, lap = laplace(now, slot, b)
            at = block_rows(b)
            at8 = block_rows(b, 8)
            before = old[at8, :]
            new = 2.0 * here - before + cw[at, :] * (lap + amplitude * hit[at, :])
            new = with_strips(b, moment, new)
            at256 = block_rows(b, 2 * TILE)
            step = (before - 2.0 * here + new) * adjoint_now[at8, :]
            old[at8, :] = new
            if moment == 0:
                grad[at, :] = step
                light[at256, :] = here * here
            else:
                grad[at, :] = grad[at, :] + step
                light[at256, :] = light[at256, :] + here * here + new * new
                turned_u[:, columns(b)] = jnp.transpose(new)
            return carry

        lax.fori_loop(0, AMAX, body, 0)

    def last_step(now, old, moment, adjoint_now):
        amplitude = wavelet[0, moment]

        def body(b, carry):
            here, lap = laplace(now, None, b)
            at = block_rows(b)
            at8 = block_rows(b, 8)
            before = old[at8, :]
            new = 2.0 * here - before + cw[at, :] * (lap + amplitude * hit[at, :])
            new = with_strips(b, moment, new)
            free = cw[at, :]
            row_here = row + b * TILE
            for i in range(2):
                free = jnp.where(row_here == low * TILE + i, 0.0, free)
                free = jnp.where(row_here == high * TILE - 2 + i, 0.0, free)
            ahead = adjoint_now[at8, :]
            known_part = grad[at, :] + (before - 2.0 * here + new) * ahead
            whole[:, columns(b, 2 * TILE)] = jnp.transpose(known_part)
            slope[:, columns(b)] = jnp.transpose(free * ahead)
            return carry

        lax.fori_loop(0, AMAX, body, 0)

    def adjoint_step(now, old, slot, moment):
        def body(b, carry):
            here, lap = laplace(now, slot, b)
            at = block_rows(b)
            at8 = block_rows(b, 8)
            old[at8, :] = 2.0 * here - old[at8, :] + cw[at, :] * (lap + inj[moment, at, :])
            return carry

        lax.fori_loop(0, AMAX, body, 0)

    u0, r0, u1, r1 = halo(ua, 0), halo(ra, 1), halo(ub, 2), halo(rb, 3)
    u2 = [halo_turned(k) for k in range(QUARTERS)]
    u0.start()
    greet(0)
    greet(1)
    loads[1].wait()
    load_block([(source, (1,), ub, 8)])

    @pl.when(pen == 0)
    def _():
        from_low[...] = jnp.zeros_like(from_low)
        low_turned[...] = jnp.zeros_like(low_turned)

    @pl.when(pen == PLANES - 1)
    def _():
        from_high[...] = jnp.zeros_like(from_high)
        high_turned[...] = jnp.zeros_like(high_turned)

    loads[2].wait()
    load_block([(adjoint, (0,), ra, 8), (adjoint, (1,), rb, 8)])
    u0.sent()
    r0.start()
    for load in loads[3:]:
        load.wait()
    greeted(0)
    greeted(1)
    greet(2)
    greet(3)
    load_block([(courant, (), cw, 0)])

    cell_row = jnp.where(cells[pl.ds(0, 1), :] == pen, cells[pl.ds(1, 1), :] - start, -1)
    slab = lax.broadcasted_iota(jnp.int32, (8, NREC), 0)
    values = jnp.where(lax.rem(slab, 2) == 0, residuals[0], residuals[1])
    coarse = values.astype(jnp.bfloat16).astype(jnp.float32)
    middle = (values - coarse).astype(jnp.bfloat16).astype(jnp.float32)
    fine = values - coarse - middle
    values = jnp.where(slab < DEPTH + 2, coarse, jnp.where(slab < DEPTH + 4, middle, fine))
    values = jnp.where(slab < DEPTH, 0.0, values)
    values = jnp.concatenate([values, jnp.zeros((NZ - 8, NREC), jnp.float32)], axis=0)
    values = jnp.transpose(values).astype(jnp.bfloat16)
    rows_wide = lax.broadcasted_iota(jnp.int32, (TILE, NREC), 0)

    def inject_block(b, carry):
        chosen = jnp.where(rows_wide == cell_row - b * TILE, 1.0, 0.0).astype(jnp.bfloat16)
        out = jnp.dot(chosen, values, preferred_element_type=jnp.float32)
        out = out + pltpu.roll(out, NZ - 2, 1) + pltpu.roll(out, NZ - 4, 1)
        at = block_rows(b)
        inj[0, at, :] = jnp.where(lane == DEPTH, out, 0.0)
        inj[1, at, :] = jnp.where(lane == DEPTH, pltpu.roll(out, NZ - 1, 1), 0.0)
        key = row + (b * TILE + pen * NY)
        cell = source_cell[0, 0] * NY + source_cell[0, 1] - start
        here = (key == cell) & (lane == source_cell[0, 2])
        hit[at, :] = jnp.where(here, 1.0, 0.0)
        return carry

    lax.fori_loop(0, AMAX, inject_block, 0)
    light[pl.ds(0, 2 * TILE), :] = jnp.zeros((2 * TILE, NZ), jnp.float32)
    light[pl.ds(ROWS + 2 * TILE, 2 * TILE), :] = jnp.zeros((2 * TILE, NZ), jnp.float32)
    whole[:, pl.ds(0, 2 * TILE)] = jnp.zeros((NZ, 2 * TILE), jnp.float32)
    whole[:, pl.ds(ROWS + 2 * TILE, 2 * TILE)] = jnp.zeros((NZ, 2 * TILE), jnp.float32)
    greeted(2)
    greeted(3)
    greet(4)

    def spread_light():
        def body(g, carry):
            options = []
            for shift in range(SHIFTS):
                options.append(light[block_rows(g, (SHIFTS - 1 - shift) * TILE), :])
            flat = jnp.transpose(pick(options, row))
            for d in range(SHOTS):
                k, j = d // 4, d % 4
                split_l[k, j, :, columns(g)] = flat[8 * d : 8 * d + 8]
            return carry

        lax.fori_loop(0, NY // TILE, body, 0)

    def spread_quarter(k):
        at = pl.ds(k * DEEP, DEEP)
        inner = pl.ds(2 * TILE, ROWS)
        pushed = low_turned[at, :] + high_turned[at, :]
        whole[at, inner] = whole[at, inner] + slope[at, :] * pushed
        for j in range(4):
            rows8 = pl.ds(k * DEEP + 8 * j, 8)
            options = []
            for shift in range(SHIFTS):
                options.append(whole[rows8, pl.ds((SHIFTS - 1 - shift) * TILE, NY)])
            like = lax.broadcasted_iota(jnp.int32, (8, NY), 0)
            split_g[k, j] = pick(options, like)

    class Sum:
        def __init__(self, split, pair, mine, ring, which):
            self.split, self.pair, self.mine, self.ring = split, pair, mine, ring
            self.pairs, self.targets = [], []
            for k in range(QUARTERS):
                self.pairs.append(
                    pltpu.make_async_remote_copy(
                        split.at[k], pair.at[k // 2], pair_send.at[which, k],
                        pair_recv.at[which, k],
                        device_id=shot_at(0, 1), device_id_type=MESH,
                    )
                )
                for j in range(4):
                    target = k // 2 + 2 * j
                    slot = lax.rem(target - z + 2 * LAYERS - 1, LAYERS)
                    copy = pltpu.make_async_remote_copy(
                        mine.at[k // 2, j], ring.at[slot], ring_send.at[which, target],
                        ring_recv.at[which, slot],
                        device_id=(2 * target + k % 2, pen), device_id_type=MESH,
                    )
                    self.targets.append(((core == k % 2) & (z != target), copy))
            self.arrivals = [
                pltpu.make_async_remote_copy(
                    mine.at[0, 0], ring.at[slot], ring_send.at[which, 0],
                    ring_recv.at[which, slot],
                    device_id=shot_at(1, 0), device_id_type=MESH,
                )
                for slot in range(LAYERS - 1)
            ]

        def start_pair(self, k):
            pl.when(core != k % 2)(self.pairs[k].start)

        def start_ring(self, k):
            @pl.when(core == k % 2)
            def _():
                self.pairs[k].wait_recv()
                self.mine[k // 2] = self.split[k] + self.pair[k // 2]

            for there, copy in self.targets[4 * k : 4 * k + 4]:
                pl.when(there)(copy.start)

        def finish(self):
            total_here = self.mine[lax.rem(z, 2), z // 2]
            for slot in range(LAYERS - 1):
                self.arrivals[slot].wait_recv()
                total_here = total_here + self.ring[slot]
            for there, copy in self.targets:
                pl.when(there)(copy.wait_send)
            for k in range(QUARTERS):
                pl.when(core != k % 2)(self.pairs[k].wait_send)
            return total_here

    sum_l = Sum(split_l, pair_l, mine_l, ring_l, 0)
    sum_g = Sum(split_g, pair_g, mine_g, ring_g, 1)

    u0.arrived()
    source_step(ua, ub, 0, 0, ra)
    r0.sent()
    u1.start()
    greeted(4)
    r0.arrived()
    adjoint_step(ra, rb, 1, 0)
    u1.sent()
    r1.start()

    def cut_block(g, carry):
        at = block_rows(g)
        waves_cut[at, :] = jnp.concatenate(cut_in_two(table[at, :]), axis=1)
        return carry

    lax.fori_loop(0, NY // TILE, cut_block, 0)
    z_cut[...] = jnp.concatenate(cut_in_two(table[pl.ds(NY, NZ), :]), axis=1)
    rows_here = pl.ds(pl.multiple_of(shot * CHUNK, CHUNK), CHUNK)
    mine_cut[...] = jnp.concatenate(cut_in_two(table[rows_here, :]), axis=0)
    u1.arrived()
    source_step(ub, ua, 2, 1, rb)
    spread_light()
    for k in range(QUARTERS):
        sum_l.start_pair(k)
    for k in range(QUARTERS):
        sum_l.start_ring(k)
    r1.sent()
    u2[0].start()
    u2[1].start()
    r1.arrived()
    adjoint_step(rb, ra, 3, 1)
    u2[0].sent()
    u2[2].start()
    last_step(ua, ub, 2, ra)
    u2[1].sent()
    u2[3].start()
    for k in range(QUARTERS):
        u2[k].arrived()
        spread_quarter(k)
        sum_g.start_pair(k)
        if k > 0:
            sum_g.start_ring(k - 1)
    sum_g.start_ring(QUARTERS - 1)
    for k in range(2, QUARTERS):
        u2[k].sent()
    lighting = sum_l.finish()
    gradient = sum_g.finish()
    precond = gradient / (lighting + DAMPING)
    for h in range(LAYERS):
        tiles[h] = precond[:, h * TILE : (h + 1) * TILE]

    def over_layers(origin, place, send, recv):
        copies = []
        for i, d in enumerate((4, 3, 5, 2, 6, 1, 7)):
            copies.append(
                pltpu.make_async_remote_copy(
                    origin(lax.rem(z + d, LAYERS)), place.at[core, z], send.at[i], recv.at[i],
                    device_id=shot_at(d, 0), device_id_type=MESH,
                )
            )
        return copies

    def to_partner(place, send, recv):
        return pltpu.make_async_remote_copy(
            place.at[core], place.at[core], send.at[LAYERS - 1], recv.at[LAYERS - 1],
            device_id=shot_at(0, 1), device_id_type=MESH,
        )

    tile_copies = over_layers(lambda layer: tiles.at[layer], tiles_in, tiles_send, tiles_recv)
    tile_pair = to_partner(tiles_in, tiles_send, tiles_recv)
    tally = jnp.dot(
        jnp.concatenate(cut_in_two(precond), axis=0),
        waves_cut[...],
        preferred_element_type=jnp.float32,
    )
    tally = four_sums(tally, 8)
    coef[...] = tally
    copies = []
    for i, rel in enumerate(PEN_REL):
        copies.append(
            pltpu.make_async_remote_copy(
                coef, coef_in.at[i], coef_send.at[i], coef_recv.at[i],
                device_id=pen_peer(rel), device_id_type=MESH,
            )
        )
    for copy in copies:
        copy.start()
    for copy in tile_copies:
        copy.start()
    tiles_in[core, z] = tiles[z]

    def share(origin):
        return table[pl.ds(NY + NZ + 8 + pen * PLANES + origin, 1), :]

    mixed = tally * share(pen)
    for i, (dy, dx) in enumerate(PEN_REL):
        copies[i].wait_recv()
        origin = lax.rem(py + SIDE - dy, SIDE) * SIDE + lax.rem(px + SIDE - dx, SIDE)
        mixed = mixed + coef_in[i] * share(origin)
    coef_copies = copies
    total[core, z] = mixed * table[pl.ds(NY + NZ, 8), :]
    copies = []
    for i, (dz, dc) in enumerate(SHOT_REL):
        copies.append(
            pltpu.make_async_remote_copy(
                total.at[core, z], total.at[core, z], total_send.at[i], total_recv.at[i],
                device_id=shot_at(dz, dc), device_id_type=MESH,
            )
        )
    for copy in copies:
        copy.start()
    for copy in tile_copies:
        copy.wait_recv()
    tile_pair.start()
    for copy in coef_copies + tile_copies:
        copy.wait_send()
    tile_pair.wait()
    stack = []
    for d in range(SHOTS):
        stack.append(tiles_in[(d // 4) % 2, d // 8 + 2 * (d % 4)])
    turned[...] = jnp.transpose(jnp.concatenate(stack, axis=0))
    both_out[0] = turned[pl.ds(pl.multiple_of(core * CHUNK, CHUNK), CHUNK), :]
    for copy in copies:
        copy.wait_recv()
    wide = lax.dot_general(
        mine_cut[...],
        jnp.concatenate(cut_in_two(total[...].reshape(NZ, MODES)), axis=0),
        (((1,), (1,)), ((), ())),
        preferred_element_type=jnp.float32,
    )
    wide = four_sums(wide, CHUNK)
    smooth = jnp.dot(
        jnp.concatenate(cut_in_two(wide), axis=0),
        z_cut[...],
        preferred_element_type=jnp.float32,
    )
    both_out[1] = four_sums(smooth, CHUNK)
    for copy in copies:
        copy.wait_send()


def on_device(
    courant,
    source_states,
    adjoint_states,
    strips,
    aperture,
    source_cell,
    wavelet,
    receiver_cells,
    residuals,
):
    table = operator_table()
    vmem = pl.BlockSpec(memory_space=pltpu.VMEM)
    hbm = pl.BlockSpec(memory_space=pltpu.HBM)
    smem = pl.BlockSpec(memory_space=pltpu.SMEM)
    f32 = jnp.float32
    dma = pltpu.SemaphoreType.DMA
    others = SHOTS - 1
    state = pltpu.VMEM((ROWS + 16, NZ), f32)
    field = pltpu.VMEM((ROWS, NZ), f32)
    both = pl.pallas_call(
        kernel,
        out_shape=jax.ShapeDtypeStruct((2, CHUNK, NZ), f32),
        in_specs=[smem] * 3 + [hbm] * 7,
        out_specs=vmem,
        scratch_shapes=[
            pltpu.VMEM((NY, NZ), f32),
            pltpu.VMEM((2, NY, NZ), f32),
            pltpu.VMEM((2, NY, NZ), f32),
            pltpu.VMEM((STEPS, 2, 2, NZ), f32),
            pltpu.VMEM((2, NREC), jnp.int32),
            pltpu.VMEM((STEPS, 1, NREC), f32),
            pltpu.VMEM(table.shape, f32),
            state,
            state,
            state,
            state,
            field,
            field,
            pltpu.VMEM((2, ROWS, NZ), f32),
            pltpu.VMEM((4, ROWS, NZ), f32),
            pltpu.VMEM((4, ROWS, NZ), f32),
            field,
            pltpu.VMEM((ROWS + 4 * TILE, NZ), f32),
            pltpu.VMEM((NZ, ROWS), f32),
            pltpu.VMEM((NZ, ROWS), f32),
            pltpu.VMEM((NZ, ROWS), f32),
            pltpu.VMEM((NZ, ROWS), f32),
            pltpu.VMEM((NZ, ROWS + 4 * TILE), f32),
            pltpu.VMEM((QUARTERS, 4, 8, NY), f32),
            pltpu.VMEM((QUARTERS, 4, 8, NY), f32),
            pltpu.VMEM((2, 4, 8, NY), f32),
            pltpu.VMEM((2, 4, 8, NY), f32),
            pltpu.VMEM((2, 4, 8, NY), f32),
            pltpu.VMEM((2, 4, 8, NY), f32),
            pltpu.VMEM((LAYERS, 8, NY), f32),
            pltpu.VMEM((LAYERS, 8, NY), f32),
            pltpu.VMEM((LAYERS, 8, TILE), f32),
            pltpu.VMEM((2, LAYERS, 8, TILE), f32),
            pltpu.VMEM((TILE, NZ), f32),
            pltpu.VMEM((8, NZ), f32),
            pltpu.VMEM((others, 8, NZ), f32),
            pltpu.VMEM((2, LAYERS, 8, NZ), f32),
            pltpu.VMEM((NY, 2 * MODES), jnp.bfloat16),
            pltpu.VMEM((2 * CHUNK, MODES), jnp.bfloat16),
            pltpu.VMEM((NZ, 2 * NZ), jnp.bfloat16),
            pltpu.SemaphoreType.REGULAR((5,)),
            dma((8,)),
            dma((QUARTERS, 2)),
            dma((QUARTERS, 2)),
            dma((4, 2)),
            dma((4, 2)),
            dma((2, QUARTERS)),
            dma((2, QUARTERS)),
            dma((2, LAYERS)),
            dma((2, LAYERS)),
            dma((LAYERS,)),
            dma((LAYERS,)),
            dma((others,)),
            dma((others,)),
            dma((others,)),
            dma((others,)),
        ],
        compiler_params=pltpu.CompilerParams(
            collective_id=0, has_side_effects=True, vmem_limit_bytes=63 << 20
        ),
        name="inversion",
    )(
        aperture,
        source_cell,
        wavelet,
        courant[0],
        source_states[0, :, 0],
        adjoint_states[0, :, 0],
        strips[0, :, :, 0],
        receiver_cells[0].T,
        residuals.transpose(1, 0, 2),
        jnp.asarray(table),
    )
    return (both[0:1], both[1:2])


def solution(mesh):
    placed = (
        P("pen", None, None),
        P("shot", None, "pen", None, None),
        P("shot", None, "pen", None, None),
        P("shot", None, None, "pen", None, None),
        P("shot", None),
        P("shot", None),
        P("shot", None),
        P("shot", None, None),
        P("shot", None, None),
    )
    return jax.shard_map(
        on_device,
        mesh=mesh,
        in_specs=placed,
        out_specs=(P("pen", "shot", None), P("pen", "shot", None)),
        check_vma=False,
    )
```
